32 devices in a mesh: head: 2 (over x), tok: 16 (over z, y, core).
Axes of the slice: x: 2, y: 2, z: 4, core: 2. Of those that a mesh axis runs over, the one named last changes fastest.
Arguments:
- queries: bfloat16 [3072, 1024], P('tok', 'head'), may hold values from -512 to 512
- keys: bfloat16 [3072, 1024], P('tok', 'head'), may hold values from -8 to 8
- values: bfloat16 [3072, 1024], P('tok', 'head'), may hold values from -6 to 6
- out_grad: bfloat16 [3072, 1024], P('tok', 'head'), may hold values from -6 to 6
- w_query: bfloat16 [1024, 1024], P(None, 'head'), may hold values from -0.1875 to 0.1875
- w_key: bfloat16 [1024, 1024], P(None, 'head'), may hold values from -0.1875 to 0.1875
- w_value: bfloat16 [1024, 1024], P(None, 'head'), may hold values from -0.1875 to 0.1875
- w_out: bfloat16 [1024, 1024], P('head'), may hold values from -0.1875 to 0.1875
- page_cluster: int32 [96], replicated, may hold values from 0 to 15, as said below
Outputs:
- input_grad: bfloat16 [3072, 1024], P('tok', 'head')
The draws below stay inside these ranges and needn't reach their ends.
Inputs may be any that keep to these rules, and one draw needn't show every extreme that they name: `page_cluster`: the 6 pages k * 6 to k * 6 + 5, for each k, name distinct clusters. No cluster is named by more than 8 pages, and some cluster by exactly 8.
All inputs are finite; a program needn't handle non-finite values.
Results may differ from the reference program's by a relative error of at most 0.014.
Values may be sent and summed in bfloat16 or wider, within the bound.
A program may use at most 64 MiB of HBM per device.

```python
import jax
import jax.numpy as jnp
from jax import lax

D = 1024
HEADS = 8
HEAD_DIM = 128
PAGE = 32
PAGES_DEV = 6
CLUSTER_PAGES = 8
TOKENS = 3072
CLUSTERS = 16
CLUSTER = 256
N_HEAD = 2


def draw_page_cluster(key, part):
    clusters = CLUSTERS
    per_device = PAGES_DEV
    donors = CLUSTER_PAGES - per_device
    sorted_label = jnp.arange(clusters, dtype=jnp.int32)
    counts = jnp.where(sorted_label == 0, CLUSTER_PAGES, jnp.where(sorted_label <= donors, per_device - 1, per_device))
    offset = sorted_label - (donors + 1)
    pair_index = jnp.maximum(offset, 0) // 2
    amount_cap = min(per_device - 1, CLUSTER_PAGES - per_device)
    amounts = jax.random.randint(jax.random.fold_in(key, 3), (clusters,), 0, amount_cap + 1)
    amount = amounts[pair_index]
    direction = jnp.where(offset < 0, 0, jnp.where(offset % 2 == 0, jnp.where(sorted_label + 1 < clusters, 1, 0), -1))
    counts = counts + direction * amount
    run_ends = jnp.cumsum(counts)
    entry_order = jnp.arange(clusters * per_device, dtype=jnp.int32)
    entry_label = jnp.sum((run_ends[None, :] <= entry_order[:, None]).astype(jnp.int32), axis=1)
    shuffle = jax.random.permutation(jax.random.fold_in(key, 5), clusters)
    chosen = shuffle[entry_label].reshape(per_device, clusters)
    rotation = jax.random.randint(jax.random.fold_in(key, 4), (), 0, clusters)
    chosen = jnp.roll(chosen, rotation, axis=1)
    return chosen.T.reshape(clusters * per_device).astype(jnp.int32)


def drawn_normal(key, shape):
    return jnp.clip(jax.random.normal(key, shape, jnp.float32), -6.0, 6.0)


def draw_keys(key, part):
    drawn = drawn_normal(jax.random.fold_in(key, 7), (TOKENS, HEADS * HEAD_DIM))
    return drawn.astype(jnp.bfloat16)


def draw_queries(key, part):
    drawn = drawn_normal(jax.random.fold_in(key, 9), (TOKENS, HEADS * HEAD_DIM))
    return drawn.astype(jnp.bfloat16)


def level_of(key, dims, shards, smallest, top_value):
    def one(dim, parts):
        heights = jax.random.uniform(jax.random.fold_in(jax.random.fold_in(key, 6), dim), (parts,), jnp.float32, smallest / len(shards), top_value / len(shards))
        return jnp.repeat(jnp.exp(heights), dims[dim] // parts).reshape((-1,) + (1,) * (len(dims) - dim - 1))

    gain = one(*shards[0])
    for cut in shards[1:]:
        gain = gain * one(*cut)
    return gain


def bell_draw(rng, shape, scale, reach, shards=(), held_as=jnp.bfloat16):
    values = scale * jax.random.normal(rng, shape, jnp.float32)
    if shards:
        values = values * level_of(rng, shape, shards, -0.22, 0.18)
    return jnp.clip(values, -reach, reach).astype(held_as)


def setup_inputs(seed: int = 0) -> dict:
    seeds = jax.random.split(jax.random.key(seed), 10)
    return {
        "queries": draw_queries(jax.random.fold_in(seeds[9], 71), 0),
        "keys": draw_keys(jax.random.fold_in(seeds[9], 71), 0),
        "values": bell_draw(seeds[2], (TOKENS, HEADS * HEAD_DIM), 1.0, 6.0, ((0, 16), (1, 2))),
        "out_grad": bell_draw(seeds[3], (TOKENS, D), 1.0, 6.0, ((0, 16), (1, 2))),
        "w_query": bell_draw(seeds[4], (D, HEADS * HEAD_DIM), D ** -0.5, 0.1875, ((1, 2),)),
        "w_key": bell_draw(seeds[5], (D, HEADS * HEAD_DIM), D ** -0.5, 0.1875, ((1, 2),)),
        "w_value": bell_draw(seeds[6], (D, HEADS * HEAD_DIM), D ** -0.5, 0.1875, ((1, 2),)),
        "w_out": bell_draw(seeds[7], (HEADS * HEAD_DIM, D), (HEADS * HEAD_DIM) ** -0.5, 0.1875, ((0, 2),)),
        "page_cluster": draw_page_cluster(jax.random.fold_in(seeds[9], 71), 0),
    }


def page_ranks(page_cluster):
    page_order = jnp.arange(page_cluster.shape[0], dtype=jnp.int32)
    same_cluster = page_cluster[:, None] == page_cluster[None, :]
    earlier = page_order[None, :] < page_order[:, None]
    return jnp.sum((same_cluster & earlier).astype(jnp.int32), axis=1)


def slot_tables(page_cluster, page_rank):
    page_order = jnp.arange(page_cluster.shape[0], dtype=jnp.int32)
    cluster_order = jnp.arange(CLUSTERS, dtype=jnp.int32)
    slot_order = jnp.arange(CLUSTER_PAGES, dtype=jnp.int32)
    slot_hit = (page_cluster[None, None, :] == cluster_order[:, None, None]) & (page_rank[None, None, :] == slot_order[None, :, None])
    filled = jnp.any(slot_hit, axis=2)
    slot_page = jnp.sum(slot_hit.astype(jnp.int32) * page_order[None, None, :], axis=2).astype(jnp.int32)
    return slot_page, filled


def head_backward(query_head, key_head, value_head, grad_head, page_cluster, slot_page, filled):
    page_total = TOKENS // PAGE
    query_pages = query_head.reshape(page_total, PAGE, HEAD_DIM)
    key_pages = key_head.reshape(page_total, PAGE, HEAD_DIM)
    value_pages = value_head.reshape(page_total, PAGE, HEAD_DIM)
    grad_pages = grad_head.reshape(page_total, PAGE, HEAD_DIM)
    inner_index = jnp.arange(PAGE, dtype=jnp.int32)
    score_scale = HEAD_DIM ** -0.5

    def page_step(running, page_number):
        dkey_sum, dvalue_sum = running
        cluster_id = page_cluster[page_number]
        key_list = slot_page[cluster_id]
        key_valid = filled[cluster_id]
        query_rows = query_pages[page_number].astype(jnp.float32)
        grad_rows = grad_pages[page_number].astype(jnp.float32)
        key_rows = key_pages[key_list].reshape(CLUSTER, HEAD_DIM).astype(jnp.float32)
        value_rows = value_pages[key_list].reshape(CLUSTER, HEAD_DIM).astype(jnp.float32)
        query_pos = page_number * PAGE + inner_index
        key_pos = (key_list[:, None] * PAGE + inner_index[None, :]).reshape(CLUSTER)
        key_live = jnp.broadcast_to(key_valid[:, None], (CLUSTER_PAGES, PAGE)).reshape(CLUSTER)
        allowed = key_live[None, :] & (key_pos[None, :] <= query_pos[:, None])
        score = jnp.dot(query_rows, key_rows.T, preferred_element_type=jnp.float32) * score_scale
        score = jnp.where(allowed, score, -1e30)
        row_max = jnp.max(score, axis=1, keepdims=True)
        raised = jnp.where(allowed, jnp.exp(score - row_max), 0.0)
        weights = raised / jnp.sum(raised, axis=1, keepdims=True)
        weights_half = lax.optimization_barrier(weights.astype(jnp.bfloat16)).astype(jnp.float32)
        grad_weights = jnp.dot(grad_rows, value_rows.T, preferred_element_type=jnp.float32)
        row_delta = jnp.sum(weights * grad_weights, axis=1, keepdims=True)
        grad_score = lax.optimization_barrier((weights * (grad_weights - row_delta)).astype(jnp.bfloat16)).astype(jnp.float32)
        dquery = (jnp.dot(grad_score, key_rows, preferred_element_type=jnp.float32) * score_scale).astype(jnp.bfloat16)
        dkey_part = jnp.dot(grad_score.T, query_rows, preferred_element_type=jnp.float32) * score_scale
        dvalue_part = jnp.dot(weights_half.T, grad_rows, preferred_element_type=jnp.float32)
        dkey_sum = dkey_sum.at[key_list].add(dkey_part.reshape(CLUSTER_PAGES, PAGE, HEAD_DIM))
        dvalue_sum = dvalue_sum.at[key_list].add(dvalue_part.reshape(CLUSTER_PAGES, PAGE, HEAD_DIM))
        return (dkey_sum, dvalue_sum), dquery

    start_sums = (jnp.zeros((page_total, PAGE, HEAD_DIM), jnp.float32), jnp.zeros((page_total, PAGE, HEAD_DIM), jnp.float32))
    sums, dquery = lax.scan(page_step, start_sums, jnp.arange(page_total, dtype=jnp.int32))
    dkey = sums[0].reshape(TOKENS, HEAD_DIM).astype(jnp.bfloat16)
    dvalue = sums[1].reshape(TOKENS, HEAD_DIM).astype(jnp.bfloat16)
    return dquery.reshape(TOKENS, HEAD_DIM), dkey, dvalue


def reference(queries, keys, values, out_grad, w_query, w_key, w_value, w_out, page_cluster):
    grad_heads = jnp.dot(out_grad, w_out.T, preferred_element_type=jnp.float32).astype(jnp.bfloat16)
    page_rank = page_ranks(page_cluster)
    slot_page, filled = slot_tables(page_cluster, page_rank)

    def split_heads(matrix):
        return matrix.reshape(TOKENS, HEADS, HEAD_DIM).transpose(1, 0, 2)

    def join_heads(matrix):
        return matrix.transpose(1, 0, 2).reshape(TOKENS, HEADS * HEAD_DIM)

    def one_head(items):
        return head_backward(items[0], items[1], items[2], items[3], page_cluster, slot_page, filled)

    stacked = (split_heads(queries), split_heads(keys), split_heads(values), split_heads(grad_heads))
    dquery, dkey, dvalue = lax.map(one_head, stacked)
    dquery = join_heads(dquery)
    dkey = join_heads(dkey)
    dvalue = join_heads(dvalue)
    group_cols = (HEADS // N_HEAD) * HEAD_DIM
    total = jnp.zeros((TOKENS, D), jnp.float32)
    for group_index in range(N_HEAD):
        low = group_index * group_cols
        high = low + group_cols
        partial_value = jnp.dot(dquery[:, low:high], w_query[:, low:high].T, preferred_element_type=jnp.float32)
        partial_value = partial_value + jnp.dot(dkey[:, low:high], w_key[:, low:high].T, preferred_element_type=jnp.float32)
        partial_value = partial_value + jnp.dot(dvalue[:, low:high], w_value[:, low:high].T, preferred_element_type=jnp.float32)
        partial_value = lax.optimization_barrier(partial_value.astype(jnp.bfloat16))
        total = total + partial_value.astype(jnp.float32)
    return total.astype(jnp.bfloat16)
```

```python
import functools

import jax
import jax.numpy as jnp
from jax import lax
from jax.experimental import pallas as pl
from jax.experimental.pallas import tpu as pltpu
from jax.sharding import PartitionSpec as P

HEAD_DIM = 128
PAGE = 32


def per_device(queries, keys, values, out_grad, w_query, w_key, w_value, w_out, page_cluster):
    tok_rows, head_cols = queries.shape
    pages_here = tok_rows // PAGE
    heads_here = head_cols // HEAD_DIM
    peers = lax.axis_size("tok")
    myself = lax.axis_index("tok")
    page_total = page_cluster.shape[0]
    slot_count = peers // 2
    cluster_rows = slot_count * PAGE
    score_scale = HEAD_DIM ** (-0.5)
    grad_heads = jnp.einsum(
        "td,hd->th",
        lax.all_gather(out_grad, "head", axis=1, tiled=True),
        w_out,
        preferred_element_type=jnp.float32,
    ).astype(jnp.bfloat16)
    page_order = jnp.arange(page_total, dtype=jnp.int32)
    peer_order = jnp.arange(peers, dtype=jnp.int32)
    cluster_onehot = (page_cluster[:, None] == peer_order[None, :]).astype(jnp.int32)
    running_count = jnp.cumsum(cluster_onehot, axis=0) - cluster_onehot
    page_rank = jnp.sum(running_count * cluster_onehot, axis=1)
    my_clusters = lax.dynamic_slice_in_dim(page_cluster, myself * pages_here, pages_here)
    going = my_clusters[None, :] == peer_order[:, None]
    going_any = jnp.any(going, axis=1)
    going_index = jnp.sum(
        going.astype(jnp.int32) * jnp.arange(pages_here, dtype=jnp.int32)[None, :], axis=1
    )

    def outgoing(matrix):
        paged = matrix.reshape(pages_here, PAGE, matrix.shape[1])
        picked = jnp.take(paged, going_index, axis=0)
        return jnp.where(going_any[:, None, None], picked, jnp.zeros_like(picked))

    arrived = (
        lax.all_to_all(outgoing(queries), "tok", split_axis=0, concat_axis=0, tiled=True),
        lax.all_to_all(outgoing(keys), "tok", split_axis=0, concat_axis=0, tiled=True),
        lax.all_to_all(outgoing(values), "tok", split_axis=0, concat_axis=0, tiled=True),
        lax.all_to_all(outgoing(grad_heads), "tok", split_axis=0, concat_axis=0, tiled=True),
    )
    slot_order = jnp.arange(slot_count, dtype=jnp.int32)
    slot_hit = (page_cluster[None, :] == myself) & (page_rank[None, :] == slot_order[:, None])
    filled = jnp.any(slot_hit, axis=1)
    slot_page = jnp.sum(slot_hit.astype(jnp.int32) * page_order[None, :], axis=1)
    slot_source = slot_page // pages_here

    def assemble(matrix):
        picked = jnp.take(matrix, slot_source, axis=0)
        picked = jnp.where(filled[:, None, None], picked, jnp.zeros_like(picked))
        return picked.reshape(cluster_rows, heads_here, HEAD_DIM)

    slot_query = assemble(arrived[0])
    slot_keys = assemble(arrived[1])
    slot_values = assemble(arrived[2])
    slot_grads = assemble(arrived[3])
    inner_index = jnp.arange(PAGE, dtype=jnp.int32)
    key_pos = (slot_page[:, None] * PAGE + inner_index[None, :]).reshape(cluster_rows)
    key_live = jnp.broadcast_to(filled[:, None], (slot_count, PAGE)).reshape(cluster_rows)
    key_order = jnp.arange(cluster_rows, dtype=jnp.int32)
    block_rows = min(512, cluster_rows)
    dkey_sum = jnp.zeros((cluster_rows, heads_here, HEAD_DIM), jnp.float32)
    dvalue_sum = jnp.zeros((cluster_rows, heads_here, HEAD_DIM), jnp.float32)
    query_parts = []
    for block_index in range(cluster_rows // block_rows):
        first_row = block_index * block_rows
        last_row = first_row + block_rows
        part_query = slot_query[first_row:last_row]
        part_grads = slot_grads[first_row:last_row]
        row_pos = key_pos[first_row:last_row]
        row_order = key_order[first_row:last_row]
        allowed = key_live[None, :] & (key_pos[None, :] <= row_pos[:, None]) | (
            key_order[None, :] == row_order[:, None]
        )
        score = (
            jnp.einsum("qhd,khd->hqk", part_query, slot_keys, preferred_element_type=jnp.float32)
            * score_scale
        )
        score = jnp.where(allowed[None], score, -1e30)
        row_max = jnp.max(score, axis=2, keepdims=True)
        raised = jnp.where(allowed[None], jnp.exp(score - row_max), 0.0)
        weights = raised / jnp.sum(raised, axis=2, keepdims=True)
        weights_half = weights.astype(jnp.bfloat16)
        grad_weights = jnp.einsum(
            "qhd,khd->hqk", part_grads, slot_values, preferred_element_type=jnp.float32
        )
        row_delta = jnp.sum(weights * grad_weights, axis=2, keepdims=True)
        grad_score = (weights * (grad_weights - row_delta)).astype(jnp.bfloat16)
        grad_query = (
            jnp.einsum("hqk,khd->qhd", grad_score, slot_keys, preferred_element_type=jnp.float32)
            * score_scale
        )
        query_parts.append(grad_query.astype(jnp.bfloat16))
        dkey_sum = dkey_sum + jnp.einsum(
            "hqk,qhd->khd", grad_score, part_query, preferred_element_type=jnp.float32
        )
        dvalue_sum = dvalue_sum + jnp.einsum(
            "hqk,qhd->khd", weights_half, part_grads, preferred_element_type=jnp.float32
        )
    slot_dquery = jnp.concatenate(query_parts, axis=0).reshape(cluster_rows, head_cols)
    slot_dkey = (dkey_sum * score_scale).astype(jnp.bfloat16).reshape(cluster_rows, head_cols)
    slot_dvalue = dvalue_sum.astype(jnp.bfloat16).reshape(cluster_rows, head_cols)
    back_hit = (slot_source[None, :] == peer_order[:, None]) & filled[None, :]
    back_any = jnp.any(back_hit, axis=1)
    back_slot = jnp.sum(back_hit.astype(jnp.int32) * slot_order[None, :], axis=1)
    share_rows = w_query.shape[0] // lax.axis_size("head")
    total = jnp.einsum("dh,th->dt", w_query, slot_dquery, preferred_element_type=jnp.float32)
    total = total + jnp.einsum("dh,th->dt", w_key, slot_dkey, preferred_element_type=jnp.float32)
    total = total + jnp.einsum(
        "dh,th->dt", w_value, slot_dvalue, preferred_element_type=jnp.float32
    )
    column_share = lax.psum_scatter(
        total.astype(jnp.bfloat16), "head", scatter_dimension=0, tiled=True
    )
    column_share = column_share.reshape(share_rows, slot_count, PAGE)
    picked = jnp.take(column_share, back_slot, axis=1)
    picked = jnp.where(back_any[None, :, None], picked, jnp.zeros_like(picked))
    returned = lax.all_to_all(picked, "tok", split_axis=1, concat_axis=1, tiled=True)
    input_grad = jnp.take(returned, my_clusters, axis=1).reshape(share_rows, tok_rows).T
    return input_grad


MESH = pl.DeviceIdType.MESH
NT = (((1,), (1,)), ((), ()))
TN = (((0,), (0,)), ((), ()))


def dot(a, b, dims):
    return lax.dot_general(a, b, dims, preferred_element_type=jnp.float32)


def whole_kernel(
    sizes, slot_ref, place_ref, q_ref, k_ref, v_ref, og_ref, wq_ref, wk_ref, wv_ref, wo_ref, out_ref,
    og_mine, og_other, wq_vm, wk_vm, wv_vm, wo_vm, grads, all_q, all_k, all_v, all_g,
    slot_q, slot_k, slot_v, done_q, done_k, done_v, ret_q, ret_k, ret_v, part_out, part_in,
    load_sem, swap_send, swap_recv, fwd_send, fwd_recv, ret_send, ret_recv,
):
    peers, pages, heads, slots = sizes
    width = heads * HEAD_DIM
    rows = pages * PAGE
    scale = HEAD_DIM ** (-0.5)
    me = lax.axis_index("tok")
    group = lax.axis_index("head")
    other = 1 - group
    owners = [peers // 4 + head * (peers // 2) // heads for head in range(heads)]

    loads = [
        pltpu.make_async_copy(og_ref, og_mine, load_sem.at[0]),
        pltpu.make_async_copy(wo_ref, wo_vm, load_sem.at[1]),
        pltpu.make_async_copy(wq_ref, wq_vm, load_sem.at[2]),
        pltpu.make_async_copy(wk_ref, wk_vm, load_sem.at[3]),
        pltpu.make_async_copy(wv_ref, wv_vm, load_sem.at[4]),
    ]
    for load in loads:
        load.start()

    barrier = pltpu.get_barrier_semaphore()
    pl.semaphore_signal(barrier, inc=1, device_id={"head": other}, device_id_type=MESH)
    for peer in range(peers):
        @pl.when(me != peer)
        def _():
            pl.semaphore_signal(barrier, inc=1, device_id={"tok": peer}, device_id_type=MESH)
    zero_page = jnp.zeros((PAGE, HEAD_DIM), jnp.bfloat16)
    for full in (all_q, all_k, all_v, all_g):
        full[peers * pages] = zero_page
    pl.semaphore_wait(barrier, peers)

    og_swap = pltpu.make_async_remote_copy(
        src_ref=og_ref, dst_ref=og_other, send_sem=swap_send.at[0], recv_sem=swap_recv.at[0],
        device_id={"head": other}, device_id_type=MESH,
    )
    og_swap.start()

    fulls = (all_q, all_k, all_v, all_g)
    sources = (q_ref, k_ref, v_ref, grads)

    def forward(tensor, head):
        piece = sources[tensor].at[:, :, pl.ds(head * HEAD_DIM, HEAD_DIM)]
        spot = fulls[tensor].at[pl.ds(me * pages, pages)]
        local = pltpu.make_async_copy(piece, spot, fwd_recv.at[tensor, me])
        remote = pltpu.make_async_remote_copy(
            src_ref=piece, dst_ref=spot, send_sem=fwd_send.at[tensor, head],
            recv_sem=fwd_recv.at[tensor, me], device_id={"tok": owners[head]}, device_id_type=MESH,
        )
        return local, remote

    def send_forward(tensor):
        for head in range(heads):
            local, remote = forward(tensor, head)

            @pl.when(me == owners[head])
            def _():
                local.start()

            @pl.when(me != owners[head])
            def _():
                remote.start()

    for tensor in range(3):
        send_forward(tensor)

    loads[0].wait()
    loads[1].wait()
    here = pl.ds(pl.multiple_of(group * width, HEAD_DIM), width)
    there = pl.ds(pl.multiple_of(other * width, HEAD_DIM), width)
    grad_sum = dot(og_mine[...].reshape(rows, width), wo_vm[:, here], NT)
    og_swap.wait()
    grad_sum = grad_sum + dot(og_other[...].reshape(rows, width), wo_vm[:, there], NT)
    grads[...] = grad_sum.astype(jnp.bfloat16).reshape(pages, PAGE, width)
    send_forward(3)

    slot_sets = (slot_q, slot_k, slot_v)
    done_sets = (done_q, done_k, done_v)
    ret_sets = (ret_q, ret_k, ret_v)
    cluster_rows = slots * PAGE

    def give_back(tensor, head, peer):
        piece = done_sets[tensor].at[pl.ds(peer * pages, pages)]
        spot = ret_sets[tensor].at[:, :, pl.ds(head * HEAD_DIM, HEAD_DIM)]
        local = pltpu.make_async_copy(piece, spot, ret_recv.at[tensor, head])
        remote = pltpu.make_async_remote_copy(
            src_ref=piece, dst_ref=spot, send_sem=ret_send.at[tensor, peer],
            recv_sem=ret_recv.at[tensor, head], device_id={"tok": peer}, device_id_type=MESH,
        )
        return local, remote

    def own_head(head):
        for tensor in range(4):
            for peer in range(peers):
                piece = sources[tensor].at[:, :, pl.ds(head * HEAD_DIM, HEAD_DIM)]
                spot = fulls[tensor].at[pl.ds(peer * pages, pages)]
                if peer == owners[head]:
                    pltpu.make_async_copy(piece, spot, fwd_recv.at[tensor, peer]).wait()
                else:
                    pltpu.make_async_remote_copy(
                        src_ref=piece, dst_ref=spot, send_sem=fwd_send.at[tensor, head],
                        recv_sem=fwd_recv.at[tensor, peer], device_id={"tok": peer}, device_id_type=MESH,
                    ).wait_recv()

    for head in range(heads):
        @pl.when(me == owners[head])
        def _():
            own_head(head)

    is_owner = functools.reduce(lambda a, b: a | b, [me == owner for owner in owners])

    @pl.when(is_owner)
    def _():
        row_index = lax.broadcasted_iota(jnp.int32, (cluster_rows, cluster_rows), 0)
        col_index = lax.broadcasted_iota(jnp.int32, (cluster_rows, cluster_rows), 1)

        def cluster_step(cluster, carry):
            picks = [slot_ref[cluster * slots + slot] for slot in range(slots)]
            query, key, value, grad = [
                jnp.concatenate([full[pick] for pick in picks], axis=0) for full in fulls
            ]
            allowed = col_index <= row_index
            score = jnp.where(allowed, dot(query, key, NT) * scale, -1e30)
            row_max = jnp.max(score, axis=1, keepdims=True)
            raised = jnp.where(allowed, jnp.exp(score - row_max), 0.0)
            weights = raised * (1.0 / jnp.sum(raised, axis=1, keepdims=True))
            grad_weights = dot(grad, value, NT)
            row_delta = jnp.sum(weights * grad_weights, axis=1, keepdims=True)
            grad_score = (weights * (grad_weights - row_delta)).astype(jnp.bfloat16)
            dquery = dot(grad_score, key, (((1,), (0,)), ((), ()))) * scale
            dkey = dot(grad_score, query, TN) * scale
            dvalue = dot(weights.astype(jnp.bfloat16), grad, TN)
            spot = pl.ds(cluster * slots, slots)
            shape = (slots, PAGE, HEAD_DIM)
            slot_q[spot] = dquery.astype(jnp.bfloat16).reshape(shape)
            slot_k[spot] = dkey.astype(jnp.bfloat16).reshape(shape)
            slot_v[spot] = dvalue.astype(jnp.bfloat16).reshape(shape)
            return carry

        lax.fori_loop(0, peers, cluster_step, 0)

        def page_step(page, carry):
            place = place_ref[page]
            for slot_set, done_set in zip(slot_sets, done_sets):
                done_set[page] = slot_set[place]
            return carry

        lax.fori_loop(0, peers * pages, page_step, 0)

    def send_back(head):
        for peer in range(peers):
            for tensor in range(3):
                local, remote = give_back(tensor, head, peer)
                if peer == owners[head]:
                    local.start()
                else:
                    remote.start()

    for head in range(heads):
        @pl.when(me == owners[head])
        def _():
            send_back(head)

    for tensor in range(3):
        for head in range(heads):
            local, remote = give_back(tensor, head, owners[head])

            @pl.when(me == owners[head])
            def _():
                local.wait()

            @pl.when(me != owners[head])
            def _():
                remote.wait_recv()

    for load in loads[2:]:
        load.wait()
    grads_in = [ret[...].reshape(rows, width) for ret in ret_sets]
    weights_in = (wq_vm, wk_vm, wv_vm)

    def partial(half):
        total = dot(grads_in[0], weights_in[0][half, :], NT)
        total = total + dot(grads_in[1], weights_in[1][half, :], NT)
        return (total + dot(grads_in[2], weights_in[2][half, :], NT)).astype(jnp.bfloat16)

    part_out[...] = partial(there)
    part_swap = pltpu.make_async_remote_copy(
        src_ref=part_out, dst_ref=part_in, send_sem=swap_send.at[1], recv_sem=swap_recv.at[1],
        device_id={"head": other}, device_id_type=MESH,
    )
    part_swap.start()
    mine = partial(here).astype(jnp.float32)
    part_swap.wait()
    out_ref[...] = (mine + part_in[...].astype(jnp.float32)).astype(jnp.bfloat16)

    for head in range(heads):
        @pl.when(me != owners[head])
        def _():
            for tensor in range(4):
                forward(tensor, head)[1].wait_send()

        @pl.when(me == owners[head])
        def _():
            for peer in range(peers):
                if peer != owners[head]:
                    for tensor in range(3):
                        give_back(tensor, head, peer)[1].wait_send()


def gathered_bytes(peers, rows, heads):
    tokens = peers * rows
    slot_rows = peers * (peers // 2) * PAGE
    return (4 * tokens + 3 * slot_rows + 3 * tokens) * HEAD_DIM * 2


def per_device_fast(queries, keys, values, out_grad, w_query, w_key, w_value, w_out, page_cluster):
    rows, width = queries.shape
    pages = rows // PAGE
    heads = width // HEAD_DIM
    peers = lax.axis_size("tok")
    slots = peers // 2
    page_total = page_cluster.shape[0]
    page_order = jnp.arange(page_total, dtype=jnp.int32)
    same = page_cluster[:, None] == page_cluster[None, :]
    earlier = page_order[None, :] < page_order[:, None]
    rank = jnp.sum((same & earlier).astype(jnp.int32), axis=1)
    place = page_cluster * slots + rank
    slot_order = jnp.arange(peers * slots, dtype=jnp.int32)
    hit = place[None, :] == slot_order[:, None]
    slot_page = page_total + jnp.sum(
        jnp.where(hit, page_order[None, :] - page_total, 0), axis=1
    ).astype(jnp.int32)
    paged = (pages, PAGE, width)
    half = jnp.bfloat16
    full = pltpu.VMEM((page_total + 1, PAGE, HEAD_DIM), half)
    slotted = pltpu.VMEM((peers * slots, PAGE, HEAD_DIM), half)
    done = pltpu.VMEM((page_total, PAGE, HEAD_DIM), half)
    small = pltpu.VMEM(paged, half)
    weight = pltpu.VMEM(w_query.shape, half)
    any_space = pl.BlockSpec(memory_space=pl.ANY)
    smem = pl.BlockSpec(memory_space=pltpu.SMEM)
    return pl.pallas_call(
        functools.partial(whole_kernel, (peers, pages, heads, slots)),
        out_shape=jax.ShapeDtypeStruct((rows, width), half),
        in_specs=[smem, smem] + [any_space] * 8,
        out_specs=pl.BlockSpec(memory_space=pltpu.VMEM),
        scratch_shapes=[small, small, weight, weight, weight, pltpu.VMEM(w_out.shape, half), small]
        + [full] * 4 + [slotted] * 3 + [done] * 3 + [small] * 3
        + [pltpu.VMEM((rows, width), half)] * 2
        + [
            pltpu.SemaphoreType.DMA((5,)),
            pltpu.SemaphoreType.DMA((2,)),
            pltpu.SemaphoreType.DMA((2,)),
            pltpu.SemaphoreType.DMA((4, heads)),
            pltpu.SemaphoreType.DMA((4, peers)),
            pltpu.SemaphoreType.DMA((3, peers)),
            pltpu.SemaphoreType.DMA((3, heads)),
        ],
        compiler_params=pltpu.CompilerParams(
            collective_id=0, has_side_effects=True, vmem_limit_bytes=40 * 1024 * 1024
        ),
    )(
        slot_page, place, queries.reshape(paged), keys.reshape(paged), values.reshape(paged),
        out_grad.reshape(paged), w_query, w_key, w_value, w_out,
    )


def choose(*arrays):
    rows, width = arrays[0].shape
    heads = width // HEAD_DIM
    peers = lax.axis_size("tok")
    fits = gathered_bytes(peers, rows, heads) < 24 * 1024 * 1024
    if lax.axis_size("head") == 2 and heads > 1 and (peers // 2) % heads == 0 and fits:
        return per_device_fast(*arrays)
    return per_device(*arrays)


def solution(mesh):
    placed = (
        P("tok", "head"),
        P("tok", "head"),
        P("tok", "head"),
        P("tok", "head"),
        P(None, "head"),
        P(None, "head"),
        P(None, "head"),
        P("head", None),
        P(),
    )
    return jax.shard_map(
        choose, mesh=mesh, in_specs=placed, out_specs=P("tok", "head"), check_vma=False
    )
```

```python
import functools

import jax
import jax.numpy as jnp
from jax import lax
from jax.experimental import pallas as pl
from jax.experimental.pallas import tpu as pltpu
from jax.sharding import PartitionSpec as P

HEAD_DIM = 128
PAGE = 32
CHUNKS = 2
UNROLL = 2
VMEM_GRANT = 67043328


def per_device(queries, keys, values, out_grad, w_query, w_key, w_value, w_out, page_cluster):
    tok_rows, head_cols = queries.shape
    pages_here = tok_rows // PAGE
    heads_here = head_cols // HEAD_DIM
    peers = lax.axis_size("tok")
    myself = lax.axis_index("tok")
    page_total = page_cluster.shape[0]
    slot_count = peers // 2
    cluster_rows = slot_count * PAGE
    score_scale = HEAD_DIM ** (-0.5)
    grad_heads = jnp.einsum(
        "td,hd->th",
        lax.all_gather(out_grad, "head", axis=1, tiled=True),
        w_out,
        preferred_element_type=jnp.float32,
    ).astype(jnp.bfloat16)
    page_order = jnp.arange(page_total, dtype=jnp.int32)
    peer_order = jnp.arange(peers, dtype=jnp.int32)
    cluster_onehot = (page_cluster[:, None] == peer_order[None, :]).astype(jnp.int32)
    running_count = jnp.cumsum(cluster_onehot, axis=0) - cluster_onehot
    page_rank = jnp.sum(running_count * cluster_onehot, axis=1)
    my_clusters = lax.dynamic_slice_in_dim(page_cluster, myself * pages_here, pages_here)
    going = my_clusters[None, :] == peer_order[:, None]
    going_any = jnp.any(going, axis=1)
    going_index = jnp.sum(
        going.astype(jnp.int32) * jnp.arange(pages_here, dtype=jnp.int32)[None, :], axis=1
    )

    def outgoing(matrix):
        paged = matrix.reshape(pages_here, PAGE, matrix.shape[1])
        picked = jnp.take(paged, going_index, axis=0)
        return jnp.where(going_any[:, None, None], picked, jnp.zeros_like(picked))

    arrived = (
        lax.all_to_all(outgoing(queries), "tok", split_axis=0, concat_axis=0, tiled=True),
        lax.all_to_all(outgoing(keys), "tok", split_axis=0, concat_axis=0, tiled=True),
        lax.all_to_all(outgoing(values), "tok", split_axis=0, concat_axis=0, tiled=True),
        lax.all_to_all(outgoing(grad_heads), "tok", split_axis=0, concat_axis=0, tiled=True),
    )
    slot_order = jnp.arange(slot_count, dtype=jnp.int32)
    slot_hit = (page_cluster[None, :] == myself) & (page_rank[None, :] == slot_order[:, None])
    filled = jnp.any(slot_hit, axis=1)
    slot_page = jnp.sum(slot_hit.astype(jnp.int32) * page_order[None, :], axis=1)
    slot_source = slot_page // pages_here

    def assemble(matrix):
        picked = jnp.take(matrix, slot_source, axis=0)
        picked = jnp.where(filled[:, None, None], picked, jnp.zeros_like(picked))
        return picked.reshape(cluster_rows, heads_here, HEAD_DIM)

    slot_query = assemble(arrived[0])
    slot_keys = assemble(arrived[1])
    slot_values = assemble(arrived[2])
    slot_grads = assemble(arrived[3])
    inner_index = jnp.arange(PAGE, dtype=jnp.int32)
    key_pos = (slot_page[:, None] * PAGE + inner_index[None, :]).reshape(cluster_rows)
    key_live = jnp.broadcast_to(filled[:, None], (slot_count, PAGE)).reshape(cluster_rows)
    key_order = jnp.arange(cluster_rows, dtype=jnp.int32)
    block_rows = min(512, cluster_rows)
    dkey_sum = jnp.zeros((cluster_rows, heads_here, HEAD_DIM), jnp.float32)
    dvalue_sum = jnp.zeros((cluster_rows, heads_here, HEAD_DIM), jnp.float32)
    query_parts = []
    for block_index in range(cluster_rows // block_rows):
        first_row = block_index * block_rows
        last_row = first_row + block_rows
        part_query = slot_query[first_row:last_row]
        part_grads = slot_grads[first_row:last_row]
        row_pos = key_pos[first_row:last_row]
        row_order = key_order[first_row:last_row]
        allowed = key_live[None, :] & (key_pos[None, :] <= row_pos[:, None]) | (
            key_order[None, :] == row_order[:, None]
        )
        score = (
            jnp.einsum("qhd,khd->hqk", part_query, slot_keys, preferred_element_type=jnp.float32)
            * score_scale
        )
        score = jnp.where(allowed[None], score, -1e30)
        row_max = jnp.max(score, axis=2, keepdims=True)
        raised = jnp.where(allowed[None], jnp.exp(score - row_max), 0.0)
        weights = raised / jnp.sum(raised, axis=2, keepdims=True)
        weights_half = weights.astype(jnp.bfloat16)
        grad_weights = jnp.einsum(
            "qhd,khd->hqk", part_grads, slot_values, preferred_element_type=jnp.float32
        )
        row_delta = jnp.sum(weights * grad_weights, axis=2, keepdims=True)
        grad_score = (weights * (grad_weights - row_delta)).astype(jnp.bfloat16)
        grad_query = (
            jnp.einsum("hqk,khd->qhd", grad_score, slot_keys, preferred_element_type=jnp.float32)
            * score_scale
        )
        query_parts.append(grad_query.astype(jnp.bfloat16))
        dkey_sum = dkey_sum + jnp.einsum(
            "hqk,qhd->khd", grad_score, part_query, preferred_element_type=jnp.float32
        )
        dvalue_sum = dvalue_sum + jnp.einsum(
            "hqk,qhd->khd", weights_half, part_grads, preferred_element_type=jnp.float32
        )
    slot_dquery = jnp.concatenate(query_parts, axis=0).reshape(cluster_rows, head_cols)
    slot_dkey = (dkey_sum * score_scale).astype(jnp.bfloat16).reshape(cluster_rows, head_cols)
    slot_dvalue = dvalue_sum.astype(jnp.bfloat16).reshape(cluster_rows, head_cols)
    back_hit = (slot_source[None, :] == peer_order[:, None]) & filled[None, :]
    back_any = jnp.any(back_hit, axis=1)
    back_slot = jnp.sum(back_hit.astype(jnp.int32) * slot_order[None, :], axis=1)
    share_rows = w_query.shape[0] // lax.axis_size("head")
    total = jnp.einsum("dh,th->dt", w_query, slot_dquery, preferred_element_type=jnp.float32)
    total = total + jnp.einsum("dh,th->dt", w_key, slot_dkey, preferred_element_type=jnp.float32)
    total = total + jnp.einsum(
        "dh,th->dt", w_value, slot_dvalue, preferred_element_type=jnp.float32
    )
    column_share = lax.psum_scatter(
        total.astype(jnp.bfloat16), "head", scatter_dimension=0, tiled=True
    )
    column_share = column_share.reshape(share_rows, slot_count, PAGE)
    picked = jnp.take(column_share, back_slot, axis=1)
    picked = jnp.where(back_any[None, :, None], picked, jnp.zeros_like(picked))
    returned = lax.all_to_all(picked, "tok", split_axis=1, concat_axis=1, tiled=True)
    input_grad = jnp.take(returned, my_clusters, axis=1).reshape(share_rows, tok_rows).T
    return input_grad


MESH = pl.DeviceIdType.MESH
NT = (((1,), (1,)), ((), ()))
TN = (((0,), (0,)), ((), ()))


def dot(a, b, dims):
    return lax.dot_general(a, b, dims, preferred_element_type=jnp.float32)


def whole_kernel(
    sizes, slot_ref, place_ref, q_ref, k_ref, v_ref, og_ref, wq_ref, wk_ref, wv_ref, wo_ref, out_ref,
    og_mine, og_other, wq_vm, wk_vm, wv_vm, wo_vm, grads, all_q, all_k, all_v, all_g,
    slot_q, slot_k, slot_v, done_q, done_k, done_v, ret_q, ret_k, ret_v, part_out, part_in, mine, held, value_sum,
    load_sem, swap_send, swap_recv, fwd_send, fwd_recv, ret_send, ret_recv,
):
    peers, pages, heads, slots = sizes
    width = heads * HEAD_DIM
    rows = pages * PAGE
    scale = HEAD_DIM ** (-0.5)
    me = lax.axis_index("tok")
    group = lax.axis_index("head")
    other = 1 - group
    owners = [peers // 4 + head * (peers // 2) // heads for head in range(heads)]

    loads = [
        pltpu.make_async_copy(og_ref, og_mine, load_sem.at[0]),
        pltpu.make_async_copy(wo_ref, wo_vm, load_sem.at[1]),
        pltpu.make_async_copy(wq_ref, wq_vm, load_sem.at[2]),
        pltpu.make_async_copy(wk_ref, wk_vm, load_sem.at[3]),
        pltpu.make_async_copy(wv_ref, wv_vm, load_sem.at[4]),
    ]
    for load in loads:
        load.start()

    barrier = pltpu.get_barrier_semaphore()
    pl.semaphore_signal(barrier, inc=1, device_id={"head": other}, device_id_type=MESH)
    for peer in range(peers):
        @pl.when(me != peer)
        def _():
            pl.semaphore_signal(barrier, inc=1, device_id={"tok": peer}, device_id_type=MESH)
    zero_page = jnp.zeros((PAGE, HEAD_DIM), jnp.bfloat16)
    for full in (all_q, all_k, all_v, all_g):
        full[peers * pages] = zero_page
    pl.semaphore_wait(barrier, peers)

    og_swap = pltpu.make_async_remote_copy(
        src_ref=og_ref, dst_ref=og_other, send_sem=swap_send.at[0], recv_sem=swap_recv.at[0],
        device_id={"head": other}, device_id_type=MESH,
    )
    og_swap.start()

    fulls = (all_q, all_k, all_v, all_g)
    sources = (q_ref, k_ref, v_ref, grads)

    def forward(tensor, head):
        piece = sources[tensor].at[:, :, pl.ds(head * HEAD_DIM, HEAD_DIM)]
        spot = fulls[tensor].at[pl.ds(me * pages, pages)]
        local = pltpu.make_async_copy(piece, spot, fwd_recv.at[tensor, me])
        remote = pltpu.make_async_remote_copy(
            src_ref=piece, dst_ref=spot, send_sem=fwd_send.at[tensor, head],
            recv_sem=fwd_recv.at[tensor, me], device_id={"tok": owners[head]}, device_id_type=MESH,
        )
        return local, remote

    def send_forward(tensor):
        for head in range(heads):
            local, remote = forward(tensor, head)

            @pl.when(me == owners[head])
            def _():
                local.start()

            @pl.when(me != owners[head])
            def _():
                remote.start()

    send_forward(0)
    send_forward(1)

    loads[0].wait()
    loads[1].wait()
    here = pl.ds(pl.multiple_of(group * width, HEAD_DIM), width)
    there = pl.ds(pl.multiple_of(other * width, HEAD_DIM), width)
    grad_sum = dot(og_mine[...].reshape(rows, width), wo_vm[:, here], NT)
    og_swap.wait()
    grad_sum = grad_sum + dot(og_other[...].reshape(rows, width), wo_vm[:, there], NT)
    grads[...] = grad_sum.astype(jnp.bfloat16).reshape(pages, PAGE, width)
    send_forward(3)
    send_forward(2)

    slot_sets = (slot_q, slot_k, slot_v)
    done_sets = (done_q, done_k, done_v)
    ret_sets = (ret_q, ret_k, ret_v)
    cluster_rows = slots * PAGE

    split = pages // CHUNKS

    def give_back(tensor, chunk, head, peer):
        piece = done_sets[tensor].at[pl.ds(peer * pages + chunk * split, split)]
        spot = ret_sets[tensor].at[pl.ds(chunk * split, split), :, pl.ds(head * HEAD_DIM, HEAD_DIM)]
        local = pltpu.make_async_copy(piece, spot, ret_recv.at[tensor, chunk, head])
        remote = pltpu.make_async_remote_copy(
            src_ref=piece, dst_ref=spot, send_sem=ret_send.at[tensor, chunk, peer],
            recv_sem=ret_recv.at[tensor, chunk, head], device_id={"tok": peer}, device_id_type=MESH,
        )
        return local, remote

    def wait_tensor(tensor, head):
        for peer in range(peers):
            piece = sources[tensor].at[:, :, pl.ds(head * HEAD_DIM, HEAD_DIM)]
            spot = fulls[tensor].at[pl.ds(peer * pages, pages)]
            if peer == owners[head]:
                pltpu.make_async_copy(piece, spot, fwd_recv.at[tensor, peer]).wait()
            else:
                pltpu.make_async_remote_copy(
                    src_ref=piece, dst_ref=spot, send_sem=fwd_send.at[tensor, head],
                    recv_sem=fwd_recv.at[tensor, peer], device_id={"tok": peer}, device_id_type=MESH,
                ).wait_recv()

    def gather(full, cluster):
        return jnp.concatenate(
            [full[slot_ref[cluster * slots + slot]] for slot in range(slots)], axis=0
        )

    def scatter(slot_set, cluster, value):
        slot_set[pl.ds(cluster * slots, slots)] = value.astype(jnp.bfloat16).reshape(
            slots, PAGE, HEAD_DIM
        )

    def every_cluster(step):
        def body(index, carry):
            for lane in range(UNROLL):
                step(index * UNROLL + lane)
            return carry

        lax.fori_loop(0, peers // UNROLL, body, 0)

    def reorder(tensors):
        def body(peer, carry):
            for inner in range(pages):
                page = peer * pages + inner
                place = place_ref[page]
                for tensor in tensors:
                    done_sets[tensor][page] = slot_sets[tensor][place]
            return carry

        lax.fori_loop(0, peers, body, 0)

    def send_back(tensors, chunk, head):
        for tensor in tensors:
            for peer in range(peers):
                local, remote = give_back(tensor, chunk, head, peer)
                if peer == owners[head]:
                    local.start()
                else:
                    remote.start()

    def weigh(cluster):
        query, key = gather(all_q, cluster), gather(all_k, cluster)
        row_index = lax.broadcasted_iota(jnp.int32, (cluster_rows, cluster_rows), 0)
        col_index = lax.broadcasted_iota(jnp.int32, (cluster_rows, cluster_rows), 1)
        score = jnp.where(col_index <= row_index, dot(query, key, NT) * scale, -1e30)
        row_max = jnp.max(score, axis=1, keepdims=True)
        raised = jnp.exp(score - row_max)
        held[cluster] = raised * (1.0 / jnp.sum(raised, axis=1, keepdims=True))

    def value_step(cluster):
        scatter(slot_v, cluster, dot(held[cluster].astype(jnp.bfloat16), gather(all_g, cluster), TN))

    def score_step(cluster):
        query, key, value, grad = [gather(full, cluster) for full in fulls]
        weights = held[cluster]
        grad_weights = dot(grad, value, NT)
        row_delta = jnp.sum(weights * grad_weights, axis=1, keepdims=True)
        grad_score = (weights * (grad_weights - row_delta)).astype(jnp.bfloat16)
        scatter(slot_q, cluster, dot(grad_score, key, (((1,), (0,)), ((), ()))) * scale)
        scatter(slot_k, cluster, dot(grad_score, query, TN) * scale)

    def as_owner(todo):
        for head in range(heads):
            @pl.when(me == owners[head])
            def _():
                todo(head)

    is_owner = functools.reduce(lambda a, b: a | b, [me == owner for owner in owners])

    as_owner(lambda head: (wait_tensor(0, head), wait_tensor(1, head)))

    @pl.when(is_owner)
    def _():
        every_cluster(weigh)

    as_owner(lambda head: wait_tensor(3, head))

    @pl.when(is_owner)
    def _():
        every_cluster(value_step)
        reorder((2,))

    as_owner(lambda head: [send_back((2,), chunk, head) for chunk in range(CHUNKS)])
    as_owner(lambda head: wait_tensor(2, head))

    @pl.when(is_owner)
    def _():
        every_cluster(score_step)
        reorder((0, 1))

    as_owner(lambda head: [send_back((0, 1), chunk, head) for chunk in range(CHUNKS)])

    def wait_back(tensor, chunk):
        for head in range(heads):
            local, remote = give_back(tensor, chunk, head, owners[head])

            @pl.when(me == owners[head])
            def _():
                local.wait()

            @pl.when(me != owners[head])
            def _():
                remote.wait_recv()

    for load in loads[2:]:
        load.wait()
    chunk_rows = split * PAGE
    for chunk in range(CHUNKS):
        wait_back(2, chunk)
    value_sum[...] = dot(ret_v[...].reshape(rows, width), wv_vm[...], NT)

    swaps = []
    for chunk in range(CHUNKS):
        span = pl.ds(chunk * chunk_rows, chunk_rows)
        wait_back(0, chunk)
        wait_back(1, chunk)
        dquery = ret_q[pl.ds(chunk * split, split)].reshape(chunk_rows, width)
        dkey = ret_k[pl.ds(chunk * split, split)].reshape(chunk_rows, width)

        def partial(half):
            total = dot(dquery, wq_vm[half, :], NT) + dot(dkey, wk_vm[half, :], NT)
            return (total + value_sum[span, half]).astype(jnp.bfloat16)

        part_out[chunk] = partial(there)
        swap = pltpu.make_async_remote_copy(
            src_ref=part_out.at[chunk], dst_ref=part_in.at[chunk],
            send_sem=swap_send.at[1 + chunk], recv_sem=swap_recv.at[1 + chunk],
            device_id={"head": other}, device_id_type=MESH,
        )
        swap.start()
        swaps.append(swap)
        mine[span, :] = partial(here)
    for chunk in range(CHUNKS):
        span = pl.ds(chunk * chunk_rows, chunk_rows)
        swaps[chunk].wait()
        out_ref[span, :] = (
            mine[span, :].astype(jnp.float32) + part_in[chunk].astype(jnp.float32)
        ).astype(jnp.bfloat16)

    for head in range(heads):
        @pl.when(me != owners[head])
        def _():
            for tensor in range(4):
                forward(tensor, head)[1].wait_send()

        @pl.when(me == owners[head])
        def _():
            for peer in range(peers):
                if peer != owners[head]:
                    for tensor in range(3):
                        for chunk in range(CHUNKS):
                            give_back(tensor, chunk, head, peer)[1].wait_send()


def gathered_bytes(peers, rows, heads):
    tokens = peers * rows
    slot_rows = peers * (peers // 2) * PAGE
    weights = peers * ((peers // 2) * PAGE) ** 2 * 4
    return (7 * tokens + 3 * slot_rows) * HEAD_DIM * 2 + weights


def per_device_fast(queries, keys, values, out_grad, w_query, w_key, w_value, w_out, page_cluster):
    rows, width = queries.shape
    pages = rows // PAGE
    heads = width // HEAD_DIM
    peers = lax.axis_size("tok")
    slots = peers // 2
    page_total = page_cluster.shape[0]
    page_order = jnp.arange(page_total, dtype=jnp.int32)
    same = page_cluster[:, None] == page_cluster[None, :]
    earlier = page_order[None, :] < page_order[:, None]
    rank = jnp.sum((same & earlier).astype(jnp.int32), axis=1)
    place = page_cluster * slots + rank
    slot_order = jnp.arange(peers * slots, dtype=jnp.int32)
    hit = place[None, :] == slot_order[:, None]
    slot_page = page_total + jnp.sum(
        jnp.where(hit, page_order[None, :] - page_total, 0), axis=1
    ).astype(jnp.int32)
    paged = (pages, PAGE, width)
    half = jnp.bfloat16
    full = pltpu.VMEM((page_total + 1, PAGE, HEAD_DIM), half)
    slotted = pltpu.VMEM((peers * slots, PAGE, HEAD_DIM), half)
    done = pltpu.VMEM((page_total, PAGE, HEAD_DIM), half)
    small = pltpu.VMEM(paged, half)
    weight = pltpu.VMEM(w_query.shape, half)
    in_hbm = pl.BlockSpec(memory_space=pltpu.HBM)
    smem = pl.BlockSpec(memory_space=pltpu.SMEM)
    return pl.pallas_call(
        functools.partial(whole_kernel, (peers, pages, heads, slots)),
        out_shape=jax.ShapeDtypeStruct((rows, width), half),
        in_specs=[smem, smem] + [in_hbm] * 8,
        out_specs=pl.BlockSpec(memory_space=pltpu.VMEM),
        scratch_shapes=[small, small, weight, weight, weight, pltpu.VMEM(w_out.shape, half), small]
        + [full] * 4 + [slotted] * 3 + [done] * 3 + [small] * 3
        + [pltpu.VMEM((CHUNKS, rows // CHUNKS, width), half)] * 2
        + [
            pltpu.VMEM((rows, width), half),
            pltpu.VMEM((peers, slots * PAGE, slots * PAGE), jnp.float32),
            pltpu.VMEM((rows, w_query.shape[0]), jnp.float32),
        ]
        + [
            pltpu.SemaphoreType.DMA((5,)),
            pltpu.SemaphoreType.DMA((1 + CHUNKS,)),
            pltpu.SemaphoreType.DMA((1 + CHUNKS,)),
            pltpu.SemaphoreType.DMA((4, heads)),
            pltpu.SemaphoreType.DMA((4, peers)),
            pltpu.SemaphoreType.DMA((3, CHUNKS, peers)),
            pltpu.SemaphoreType.DMA((3, CHUNKS, heads)),
        ],
        compiler_params=pltpu.CompilerParams(
            collective_id=0, has_side_effects=True, vmem_limit_bytes=VMEM_GRANT
        ),
    )(
        slot_page, place, queries.reshape(paged), keys.reshape(paged), values.reshape(paged),
        out_grad.reshape(paged), w_query, w_key, w_value, w_out,
    )


def choose(*arrays):
    rows, width = arrays[0].shape
    heads = width // HEAD_DIM
    peers = lax.axis_size("tok")
    fits = gathered_bytes(peers, rows, heads) < 24 * 1024 * 1024
    whole_chunks = (rows // PAGE) % CHUNKS == 0 and peers % UNROLL == 0
    if lax.axis_size("head") == 2 and heads > 1 and (peers // 2) % heads == 0 and fits and whole_chunks:
        return per_device_fast(*arrays)
    return per_device(*arrays)


def solution(mesh):
    placed = (
        P("tok", "head"),
        P("tok", "head"),
        P("tok", "head"),
        P("tok", "head"),
        P(None, "head"),
        P(None, "head"),
        P(None, "head"),
        P("head", None),
        P(),
    )
    return jax.shard_map(
        choose, mesh=mesh, in_specs=placed, out_specs=P("tok", "head"), check_vma=False
    )
```

```python
import functools

import jax
import jax.numpy as jnp
from jax import lax
from jax.experimental import pallas as pl
from jax.experimental.pallas import tpu as pltpu
from jax.sharding import PartitionSpec as P

HEAD_DIM = 128
PAGE = 32
CHUNKS = 3
UNROLL = 2
VMEM_GRANT = 67043328


def per_device(queries, keys, values, out_grad, w_query, w_key, w_value, w_out, page_cluster):
    tok_rows, head_cols = queries.shape
    pages_here = tok_rows // PAGE
    heads_here = head_cols // HEAD_DIM
    peers = lax.axis_size("tok")
    myself = lax.axis_index("tok")
    page_total = page_cluster.shape[0]
    slot_count = peers // 2
    cluster_rows = slot_count * PAGE
    score_scale = HEAD_DIM ** (-0.5)
    grad_heads = jnp.einsum(
        "td,hd->th",
        lax.all_gather(out_grad, "head", axis=1, tiled=True),
        w_out,
        preferred_element_type=jnp.float32,
    ).astype(jnp.bfloat16)
    page_order = jnp.arange(page_total, dtype=jnp.int32)
    peer_order = jnp.arange(peers, dtype=jnp.int32)
    cluster_onehot = (page_cluster[:, None] == peer_order[None, :]).astype(jnp.int32)
    running_count = jnp.cumsum(cluster_onehot, axis=0) - cluster_onehot
    page_rank = jnp.sum(running_count * cluster_onehot, axis=1)
    my_clusters = lax.dynamic_slice_in_dim(page_cluster, myself * pages_here, pages_here)
    going = my_clusters[None, :] == peer_order[:, None]
    going_any = jnp.any(going, axis=1)
    going_index = jnp.sum(
        going.astype(jnp.int32) * jnp.arange(pages_here, dtype=jnp.int32)[None, :], axis=1
    )

    def outgoing(matrix):
        paged = matrix.reshape(pages_here, PAGE, matrix.shape[1])
        picked = jnp.take(paged, going_index, axis=0)
        return jnp.where(going_any[:, None, None], picked, jnp.zeros_like(picked))

    arrived = (
        lax.all_to_all(outgoing(queries), "tok", split_axis=0, concat_axis=0, tiled=True),
        lax.all_to_all(outgoing(keys), "tok", split_axis=0, concat_axis=0, tiled=True),
        lax.all_to_all(outgoing(values), "tok", split_axis=0, concat_axis=0, tiled=True),
        lax.all_to_all(outgoing(grad_heads), "tok", split_axis=0, concat_axis=0, tiled=True),
    )
    slot_order = jnp.arange(slot_count, dtype=jnp.int32)
    slot_hit = (page_cluster[None, :] == myself) & (page_rank[None, :] == slot_order[:, None])
    filled = jnp.any(slot_hit, axis=1)
    slot_page = jnp.sum(slot_hit.astype(jnp.int32) * page_order[None, :], axis=1)
    slot_source = slot_page // pages_here

    def assemble(matrix):
        picked = jnp.take(matrix, slot_source, axis=0)
        picked = jnp.where(filled[:, None, None], picked, jnp.zeros_like(picked))
        return picked.reshape(cluster_rows, heads_here, HEAD_DIM)

    slot_query = assemble(arrived[0])
    slot_keys = assemble(arrived[1])
    slot_values = assemble(arrived[2])
    slot_grads = assemble(arrived[3])
    inner_index = jnp.arange(PAGE, dtype=jnp.int32)
    key_pos = (slot_page[:, None] * PAGE + inner_index[None, :]).reshape(cluster_rows)
    key_live = jnp.broadcast_to(filled[:, None], (slot_count, PAGE)).reshape(cluster_rows)
    key_order = jnp.arange(cluster_rows, dtype=jnp.int32)
    block_rows = min(512, cluster_rows)
    dkey_sum = jnp.zeros((cluster_rows, heads_here, HEAD_DIM), jnp.float32)
    dvalue_sum = jnp.zeros((cluster_rows, heads_here, HEAD_DIM), jnp.float32)
    query_parts = []
    for block_index in range(cluster_rows // block_rows):
        first_row = block_index * block_rows
        last_row = first_row + block_rows
        part_query = slot_query[first_row:last_row]
        part_grads = slot_grads[first_row:last_row]
        row_pos = key_pos[first_row:last_row]
        row_order = key_order[first_row:last_row]
        allowed = key_live[None, :] & (key_pos[None, :] <= row_pos[:, None]) | (
            key_order[None, :] == row_order[:, None]
        )
        score = (
            jnp.einsum("qhd,khd->hqk", part_query, slot_keys, preferred_element_type=jnp.float32)
            * score_scale
        )
        score = jnp.where(allowed[None], score, -1e30)
        row_max = jnp.max(score, axis=2, keepdims=True)
        raised = jnp.where(allowed[None], jnp.exp(score - row_max), 0.0)
        weights = raised / jnp.sum(raised, axis=2, keepdims=True)
        weights_half = weights.astype(jnp.bfloat16)
        grad_weights = jnp.einsum(
            "qhd,khd->hqk", part_grads, slot_values, preferred_element_type=jnp.float32
        )
        row_delta = jnp.sum(weights * grad_weights, axis=2, keepdims=True)
        grad_score = (weights * (grad_weights - row_delta)).astype(jnp.bfloat16)
        grad_query = (
            jnp.einsum("hqk,khd->qhd", grad_score, slot_keys, preferred_element_type=jnp.float32)
            * score_scale
        )
        query_parts.append(grad_query.astype(jnp.bfloat16))
        dkey_sum = dkey_sum + jnp.einsum(
            "hqk,qhd->khd", grad_score, part_query, preferred_element_type=jnp.float32
        )
        dvalue_sum = dvalue_sum + jnp.einsum(
            "hqk,qhd->khd", weights_half, part_grads, preferred_element_type=jnp.float32
        )
    slot_dquery = jnp.concatenate(query_parts, axis=0).reshape(cluster_rows, head_cols)
    slot_dkey = (dkey_sum * score_scale).astype(jnp.bfloat16).reshape(cluster_rows, head_cols)
    slot_dvalue = dvalue_sum.astype(jnp.bfloat16).reshape(cluster_rows, head_cols)
    back_hit = (slot_source[None, :] == peer_order[:, None]) & filled[None, :]
    back_any = jnp.any(back_hit, axis=1)
    back_slot = jnp.sum(back_hit.astype(jnp.int32) * slot_order[None, :], axis=1)
    share_rows = w_query.shape[0] // lax.axis_size("head")
    total = jnp.einsum("dh,th->dt", w_query, slot_dquery, preferred_element_type=jnp.float32)
    total = total + jnp.einsum("dh,th->dt", w_key, slot_dkey, preferred_element_type=jnp.float32)
    total = total + jnp.einsum(
        "dh,th->dt", w_value, slot_dvalue, preferred_element_type=jnp.float32
    )
    column_share = lax.psum_scatter(
        total.astype(jnp.bfloat16), "head", scatter_dimension=0, tiled=True
    )
    column_share = column_share.reshape(share_rows, slot_count, PAGE)
    picked = jnp.take(column_share, back_slot, axis=1)
    picked = jnp.where(back_any[None, :, None], picked, jnp.zeros_like(picked))
    returned = lax.all_to_all(picked, "tok", split_axis=1, concat_axis=1, tiled=True)
    input_grad = jnp.take(returned, my_clusters, axis=1).reshape(share_rows, tok_rows).T
    return input_grad


MESH = pl.DeviceIdType.MESH
NT = (((1,), (1,)), ((), ()))
TN = (((0,), (0,)), ((), ()))


def dot(a, b, dims):
    return lax.dot_general(a, b, dims, preferred_element_type=jnp.float32)


def whole_kernel(
    sizes, cluster_ref, q_ref, k_ref, v_ref, og_ref, wq_ref, wk_ref, wv_ref, wo_ref, out_ref,
    og_mine, og_other, wq_vm, wk_vm, wv_vm, wo_vm, grads, all_q, all_k, all_v, all_g,
    slot_q, slot_k, slot_v, done_q, done_k, done_v, ret_q, ret_k, ret_v, part_out, part_in, mine, held, value_sum,
    cluster_vm, slot_vm, place_vm, slot_sm, place_sm,
    load_sem, swap_send, swap_recv, fwd_send, fwd_recv, ret_send, ret_recv,
):
    peers, pages, heads, slots = sizes
    width = heads * HEAD_DIM
    rows = pages * PAGE
    scale = HEAD_DIM ** (-0.5)
    me = lax.axis_index("tok")
    group = lax.axis_index("head")
    other = 1 - group
    owners = [peers // 4 + head * (peers // 2) // heads for head in range(heads)]

    loads = [
        pltpu.make_async_copy(og_ref, og_mine, load_sem.at[0]),
        pltpu.make_async_copy(wo_ref, wo_vm, load_sem.at[1]),
        pltpu.make_async_copy(wq_ref, wq_vm, load_sem.at[2]),
        pltpu.make_async_copy(wk_ref, wk_vm, load_sem.at[3]),
        pltpu.make_async_copy(wv_ref, wv_vm, load_sem.at[4]),
    ]
    cluster_load = pltpu.make_async_copy(cluster_ref, cluster_vm, load_sem.at[5])
    cluster_load.start()
    for load in loads:
        load.start()

    is_owner = functools.reduce(lambda a, b: a | b, [me == owner for owner in owners])
    barrier = pltpu.get_barrier_semaphore()
    pl.semaphore_signal(barrier, inc=1, device_id={"head": other}, device_id_type=MESH)
    for peer in range(peers):
        meets = me != peer if peer in owners else is_owner & (me != peer)

        @pl.when(meets)
        def _():
            pl.semaphore_signal(barrier, inc=1, device_id={"tok": peer}, device_id_type=MESH)

    zero_page = jnp.zeros((PAGE, HEAD_DIM), jnp.bfloat16)
    for full in (all_q, all_k, all_v, all_g):
        full[peers * pages] = zero_page
    cluster_load.wait()
    page_total = peers * pages
    square = (page_total, page_total)
    down = lax.broadcasted_iota(jnp.int32, square, 0)
    along = lax.broadcasted_iota(jnp.int32, square, 1)

    def upright(row):
        return jnp.sum(jnp.where(down == along, row, 0), axis=1, keepdims=True)

    cluster_row = cluster_vm[...]
    before = (upright(cluster_row) == cluster_row) & (down < along)
    rank_row = jnp.sum(before.astype(jnp.int32), axis=0, keepdims=True)
    place_row = cluster_row * slots + rank_row
    place_vm[...] = place_row
    shape = (page_total, peers * slots)
    hit = upright(place_row) == lax.broadcasted_iota(jnp.int32, shape, 1)
    missing = lax.broadcasted_iota(jnp.int32, shape, 0) - page_total
    slot_vm[...] = page_total + jnp.sum(jnp.where(hit, missing, 0), axis=0, keepdims=True)
    tables = [
        pltpu.make_async_copy(slot_vm, slot_sm, load_sem.at[6]),
        pltpu.make_async_copy(place_vm, place_sm, load_sem.at[7]),
    ]
    for table in tables:
        table.start()

    @pl.when(is_owner)
    def _():
        pl.semaphore_wait(barrier, peers)

    @pl.when(jnp.logical_not(is_owner))
    def _():
        pl.semaphore_wait(barrier, heads + 1)

    og_swap = pltpu.make_async_remote_copy(
        src_ref=og_ref, dst_ref=og_other, send_sem=swap_send.at[0], recv_sem=swap_recv.at[0],
        device_id={"head": other}, device_id_type=MESH,
    )
    og_swap.start()

    fulls = (all_q, all_k, all_v, all_g)
    sources = (q_ref, k_ref, v_ref, grads)

    def forward(tensor, head):
        piece = sources[tensor].at[:, :, pl.ds(head * HEAD_DIM, HEAD_DIM)]
        spot = fulls[tensor].at[pl.ds(me * pages, pages)]
        local = pltpu.make_async_copy(piece, spot, fwd_recv.at[tensor, me])
        remote = pltpu.make_async_remote_copy(
            src_ref=piece, dst_ref=spot, send_sem=fwd_send.at[tensor, head],
            recv_sem=fwd_recv.at[tensor, me], device_id={"tok": owners[head]}, device_id_type=MESH,
        )
        return local, remote

    def send_forward(tensor):
        for head in range(heads):
            local, remote = forward(tensor, head)

            @pl.when(me == owners[head])
            def _():
                local.start()

            @pl.when(me != owners[head])
            def _():
                remote.start()

    send_forward(0)
    send_forward(1)

    loads[0].wait()
    loads[1].wait()
    here = pl.ds(pl.multiple_of(group * width, HEAD_DIM), width)
    there = pl.ds(pl.multiple_of(other * width, HEAD_DIM), width)
    grad_sum = dot(og_mine[...].reshape(rows, width), wo_vm[:, here], NT)
    og_swap.wait()
    grad_sum = grad_sum + dot(og_other[...].reshape(rows, width), wo_vm[:, there], NT)
    grads[...] = grad_sum.astype(jnp.bfloat16).reshape(pages, PAGE, width)
    send_forward(3)
    send_forward(2)

    slot_sets = (slot_q, slot_k, slot_v)
    done_sets = (done_q, done_k, done_v)
    ret_sets = (ret_q, ret_k, ret_v)
    cluster_rows = slots * PAGE

    split = pages // CHUNKS

    def give_back(tensor, chunk, head, peer):
        piece = done_sets[tensor].at[pl.ds(peer * pages + chunk * split, split)]
        spot = ret_sets[tensor].at[pl.ds(chunk * split, split), :, pl.ds(head * HEAD_DIM, HEAD_DIM)]
        local = pltpu.make_async_copy(piece, spot, ret_recv.at[tensor, chunk, head])
        remote = pltpu.make_async_remote_copy(
            src_ref=piece, dst_ref=spot, send_sem=ret_send.at[tensor, chunk, peer],
            recv_sem=ret_recv.at[tensor, chunk, head], device_id={"tok": peer}, device_id_type=MESH,
        )
        return local, remote

    def wait_tensor(tensor, head):
        for peer in range(peers):
            piece = sources[tensor].at[:, :, pl.ds(head * HEAD_DIM, HEAD_DIM)]
            spot = fulls[tensor].at[pl.ds(peer * pages, pages)]
            if peer == owners[head]:
                pltpu.make_async_copy(piece, spot, fwd_recv.at[tensor, peer]).wait()
            else:
                pltpu.make_async_remote_copy(
                    src_ref=piece, dst_ref=spot, send_sem=fwd_send.at[tensor, head],
                    recv_sem=fwd_recv.at[tensor, peer], device_id={"tok": peer}, device_id_type=MESH,
                ).wait_recv()

    def gather(full, cluster):
        return jnp.concatenate(
            [full[slot_sm[0, cluster * slots + slot]] for slot in range(slots)], axis=0
        )

    def scatter(slot_set, cluster, value):
        slot_set[pl.ds(cluster * slots, slots)] = value.astype(jnp.bfloat16).reshape(
            slots, PAGE, HEAD_DIM
        )

    def every_cluster(step):
        def body(index, carry):
            for lane in range(UNROLL):
                step(index * UNROLL + lane)
            return carry

        lax.fori_loop(0, peers // UNROLL, body, 0)

    def reorder(tensors):
        def body(peer, carry):
            for inner in range(pages):
                page = peer * pages + inner
                place = place_sm[0, page]
                for tensor in tensors:
                    done_sets[tensor][page] = slot_sets[tensor][place]
            return carry

        lax.fori_loop(0, peers, body, 0)

    def send_back(tensors, chunk, head):
        for tensor in tensors:
            for peer in range(peers):
                local, remote = give_back(tensor, chunk, head, peer)
                if peer == owners[head]:
                    local.start()
                else:
                    remote.start()

    def weigh(cluster):
        query, key = gather(all_q, cluster), gather(all_k, cluster)
        row_index = lax.broadcasted_iota(jnp.int32, (cluster_rows, cluster_rows), 0)
        col_index = lax.broadcasted_iota(jnp.int32, (cluster_rows, cluster_rows), 1)
        score = jnp.where(col_index <= row_index, dot(query, key, NT) * scale, -1e30)
        row_max = jnp.max(score, axis=1, keepdims=True)
        raised = jnp.exp(score - row_max)
        held[cluster] = raised * (1.0 / jnp.sum(raised, axis=1, keepdims=True))

    def value_step(cluster):
        scatter(slot_v, cluster, dot(held[cluster].astype(jnp.bfloat16), gather(all_g, cluster), TN))

    def score_step(cluster):
        query, key, value, grad = [gather(full, cluster) for full in fulls]
        weights = held[cluster]
        grad_weights = dot(grad, value, NT)
        row_delta = jnp.sum(weights * grad_weights, axis=1, keepdims=True)
        grad_score = (weights * (grad_weights - row_delta)).astype(jnp.bfloat16)
        scatter(slot_q, cluster, dot(grad_score, key, (((1,), (0,)), ((), ()))) * scale)
        scatter(slot_k, cluster, dot(grad_score, query, TN) * scale)

    def as_owner(todo):
        for head in range(heads):
            @pl.when(me == owners[head])
            def _():
                todo(head)

    for table in tables:
        table.wait()
    as_owner(lambda head: (wait_tensor(0, head), wait_tensor(1, head)))

    @pl.when(is_owner)
    def _():
        every_cluster(weigh)

    as_owner(lambda head: wait_tensor(3, head))

    @pl.when(is_owner)
    def _():
        every_cluster(value_step)
        reorder((2,))

    as_owner(lambda head: wait_tensor(2, head))
    as_owner(lambda head: [send_back((2,), chunk, head) for chunk in range(CHUNKS)])

    @pl.when(is_owner)
    def _():
        every_cluster(score_step)
        reorder((0, 1))

    as_owner(lambda head: [send_back((0, 1), chunk, head) for chunk in range(CHUNKS)])

    def wait_back(tensor, chunk):
        for head in range(heads):
            local, remote = give_back(tensor, chunk, head, owners[head])

            @pl.when(me == owners[head])
            def _():
                local.wait()

            @pl.when(me != owners[head])
            def _():
                remote.wait_recv()

    for load in loads[2:]:
        load.wait()
    chunk_rows = split * PAGE
    for chunk in range(CHUNKS):
        wait_back(2, chunk)
    value_sum[...] = dot(ret_v[...].reshape(rows, width), wv_vm[...], NT)

    swaps = []
    for chunk in range(CHUNKS):
        span = pl.ds(chunk * chunk_rows, chunk_rows)
        wait_back(0, chunk)
        wait_back(1, chunk)
        dquery = ret_q[pl.ds(chunk * split, split)].reshape(chunk_rows, width)
        dkey = ret_k[pl.ds(chunk * split, split)].reshape(chunk_rows, width)

        def partial(half):
            total = dot(dquery, wq_vm[half, :], NT) + dot(dkey, wk_vm[half, :], NT)
            return (total + value_sum[span, half]).astype(jnp.bfloat16)

        part_out[chunk] = partial(there)
        swap = pltpu.make_async_remote_copy(
            src_ref=part_out.at[chunk], dst_ref=part_in.at[chunk],
            send_sem=swap_send.at[1 + chunk], recv_sem=swap_recv.at[1 + chunk],
            device_id={"head": other}, device_id_type=MESH,
        )
        swap.start()
        swaps.append(swap)
        mine[span, :] = partial(here)
    for chunk in range(CHUNKS):
        span = pl.ds(chunk * chunk_rows, chunk_rows)
        swaps[chunk].wait()
        out_ref[span, :] = (
            mine[span, :].astype(jnp.float32) + part_in[chunk].astype(jnp.float32)
        ).astype(jnp.bfloat16)

    for head in range(heads):
        @pl.when(me != owners[head])
        def _():
            for tensor in range(4):
                forward(tensor, head)[1].wait_send()

        @pl.when(me == owners[head])
        def _():
            for peer in range(peers):
                if peer != owners[head]:
                    for tensor in range(3):
                        for chunk in range(CHUNKS):
                            give_back(tensor, chunk, head, peer)[1].wait_send()


def gathered_bytes(peers, rows, heads):
    tokens = peers * rows
    slot_rows = peers * (peers // 2) * PAGE
    weights = peers * ((peers // 2) * PAGE) ** 2 * 4
    return (7 * tokens + 3 * slot_rows) * HEAD_DIM * 2 + weights


def per_device_fast(queries, keys, values, out_grad, w_query, w_key, w_value, w_out, page_cluster):
    rows, width = queries.shape
    pages = rows // PAGE
    heads = width // HEAD_DIM
    peers = lax.axis_size("tok")
    slots = peers // 2
    page_total = page_cluster.shape[0]
    paged = (pages, PAGE, width)
    half = jnp.bfloat16
    full = pltpu.VMEM((page_total + 1, PAGE, HEAD_DIM), half)
    slotted = pltpu.VMEM((peers * slots, PAGE, HEAD_DIM), half)
    done = pltpu.VMEM((page_total, PAGE, HEAD_DIM), half)
    small = pltpu.VMEM(paged, half)
    weight = pltpu.VMEM(w_query.shape, half)
    in_hbm = pl.BlockSpec(memory_space=pltpu.HBM)
    return pl.pallas_call(
        functools.partial(whole_kernel, (peers, pages, heads, slots)),
        out_shape=jax.ShapeDtypeStruct((rows, width), half),
        in_specs=[in_hbm] * 9,
        out_specs=pl.BlockSpec(memory_space=pltpu.VMEM),
        scratch_shapes=[small, small, weight, weight, weight, pltpu.VMEM(w_out.shape, half), small]
        + [full] * 4 + [slotted] * 3 + [done] * 3 + [small] * 3
        + [pltpu.VMEM((CHUNKS, rows // CHUNKS, width), half)] * 2
        + [
            pltpu.VMEM((rows, width), half),
            pltpu.VMEM((peers, slots * PAGE, slots * PAGE), jnp.float32),
            pltpu.VMEM((rows, w_query.shape[0]), jnp.float32),
        ]
        + [pltpu.VMEM((1, size), jnp.int32) for size in (page_total, peers * slots, page_total)]
        + [pltpu.SMEM((1, size), jnp.int32) for size in (peers * slots, page_total)]
        + [
            pltpu.SemaphoreType.DMA((8,)),
            pltpu.SemaphoreType.DMA((1 + CHUNKS,)),
            pltpu.SemaphoreType.DMA((1 + CHUNKS,)),
            pltpu.SemaphoreType.DMA((4, heads)),
            pltpu.SemaphoreType.DMA((4, peers)),
            pltpu.SemaphoreType.DMA((3, CHUNKS, peers)),
            pltpu.SemaphoreType.DMA((3, CHUNKS, heads)),
        ],
        compiler_params=pltpu.CompilerParams(
            collective_id=0, has_side_effects=True, vmem_limit_bytes=VMEM_GRANT
        ),
    )(
        page_cluster.reshape(1, page_total), queries.reshape(paged), keys.reshape(paged), values.reshape(paged),
        out_grad.reshape(paged), w_query, w_key, w_value, w_out,
    )


def choose(*arrays):
    rows, width = arrays[0].shape
    heads = width // HEAD_DIM
    peers = lax.axis_size("tok")
    fits = gathered_bytes(peers, rows, heads) < 24 * 1024 * 1024
    whole_chunks = (rows // PAGE) % CHUNKS == 0 and peers % UNROLL == 0
    if lax.axis_size("head") == 2 and heads > 1 and (peers // 2) % heads == 0 and fits and whole_chunks:
        return per_device_fast(*arrays)
    return per_device(*arrays)


def solution(mesh):
    placed = (
        P("tok", "head"),
        P("tok", "head"),
        P("tok", "head"),
        P("tok", "head"),
        P(None, "head"),
        P(None, "head"),
        P(None, "head"),
        P("head", None),
        P(),
    )
    return jax.shard_map(
        choose, mesh=mesh, in_specs=placed, out_specs=P("tok", "head"), check_vma=False
    )
```

```python
import functools

import jax
import jax.numpy as jnp
from jax import lax
from jax.experimental import pallas as pl
from jax.experimental.pallas import tpu as pltpu
from jax.sharding import PartitionSpec as P

HEAD_DIM = 128
PAGE = 32
CHUNKS = 3
UNROLL = 4
VMEM_GRANT = 67043328


def per_device(queries, keys, values, out_grad, w_query, w_key, w_value, w_out, page_cluster):
    tok_rows, head_cols = queries.shape
    pages_here = tok_rows // PAGE
    heads_here = head_cols // HEAD_DIM
    peers = lax.axis_size("tok")
    myself = lax.axis_index("tok")
    page_total = page_cluster.shape[0]
    slot_count = peers // 2
    cluster_rows = slot_count * PAGE
    score_scale = HEAD_DIM ** (-0.5)
    grad_heads = jnp.einsum(
        "td,hd->th",
        lax.all_gather(out_grad, "head", axis=1, tiled=True),
        w_out,
        preferred_element_type=jnp.float32,
    ).astype(jnp.bfloat16)
    page_order = jnp.arange(page_total, dtype=jnp.int32)
    peer_order = jnp.arange(peers, dtype=jnp.int32)
    cluster_onehot = (page_cluster[:, None] == peer_order[None, :]).astype(jnp.int32)
    running_count = jnp.cumsum(cluster_onehot, axis=0) - cluster_onehot
    page_rank = jnp.sum(running_count * cluster_onehot, axis=1)
    my_clusters = lax.dynamic_slice_in_dim(page_cluster, myself * pages_here, pages_here)
    going = my_clusters[None, :] == peer_order[:, None]
    going_any = jnp.any(going, axis=1)
    going_index = jnp.sum(
        going.astype(jnp.int32) * jnp.arange(pages_here, dtype=jnp.int32)[None, :], axis=1
    )

    def outgoing(matrix):
        paged = matrix.reshape(pages_here, PAGE, matrix.shape[1])
        picked = jnp.take(paged, going_index, axis=0)
        return jnp.where(going_any[:, None, None], picked, jnp.zeros_like(picked))

    arrived = (
        lax.all_to_all(outgoing(queries), "tok", split_axis=0, concat_axis=0, tiled=True),
        lax.all_to_all(outgoing(keys), "tok", split_axis=0, concat_axis=0, tiled=True),
        lax.all_to_all(outgoing(values), "tok", split_axis=0, concat_axis=0, tiled=True),
        lax.all_to_all(outgoing(grad_heads), "tok", split_axis=0, concat_axis=0, tiled=True),
    )
    slot_order = jnp.arange(slot_count, dtype=jnp.int32)
    slot_hit = (page_cluster[None, :] == myself) & (page_rank[None, :] == slot_order[:, None])
    filled = jnp.any(slot_hit, axis=1)
    slot_page = jnp.sum(slot_hit.astype(jnp.int32) * page_order[None, :], axis=1)
    slot_source = slot_page // pages_here

    def assemble(matrix):
        picked = jnp.take(matrix, slot_source, axis=0)
        picked = jnp.where(filled[:, None, None], picked, jnp.zeros_like(picked))
        return picked.reshape(cluster_rows, heads_here, HEAD_DIM)

    slot_query = assemble(arrived[0])
    slot_keys = assemble(arrived[1])
    slot_values = assemble(arrived[2])
    slot_grads = assemble(arrived[3])
    inner_index = jnp.arange(PAGE, dtype=jnp.int32)
    key_pos = (slot_page[:, None] * PAGE + inner_index[None, :]).reshape(cluster_rows)
    key_live = jnp.broadcast_to(filled[:, None], (slot_count, PAGE)).reshape(cluster_rows)
    key_order = jnp.arange(cluster_rows, dtype=jnp.int32)
    block_rows = min(512, cluster_rows)
    dkey_sum = jnp.zeros((cluster_rows, heads_here, HEAD_DIM), jnp.float32)
    dvalue_sum = jnp.zeros((cluster_rows, heads_here, HEAD_DIM), jnp.float32)
    query_parts = []
    for block_index in range(cluster_rows // block_rows):
        first_row = block_index * block_rows
        last_row = first_row + block_rows
        part_query = slot_query[first_row:last_row]
        part_grads = slot_grads[first_row:last_row]
        row_pos = key_pos[first_row:last_row]
        row_order = key_order[first_row:last_row]
        allowed = key_live[None, :] & (key_pos[None, :] <= row_pos[:, None]) | (
            key_order[None, :] == row_order[:, None]
        )
        score = (
            jnp.einsum("qhd,khd->hqk", part_query, slot_keys, preferred_element_type=jnp.float32)
            * score_scale
        )
        score = jnp.where(allowed[None], score, -1e30)
        row_max = jnp.max(score, axis=2, keepdims=True)
        raised = jnp.where(allowed[None], jnp.exp(score - row_max), 0.0)
        weights = raised / jnp.sum(raised, axis=2, keepdims=True)
        weights_half = weights.astype(jnp.bfloat16)
        grad_weights = jnp.einsum(
            "qhd,khd->hqk", part_grads, slot_values, preferred_element_type=jnp.float32
        )
        row_delta = jnp.sum(weights * grad_weights, axis=2, keepdims=True)
        grad_score = (weights * (grad_weights - row_delta)).astype(jnp.bfloat16)
        grad_query = (
            jnp.einsum("hqk,khd->qhd", grad_score, slot_keys, preferred_element_type=jnp.float32)
            * score_scale
        )
        query_parts.append(grad_query.astype(jnp.bfloat16))
        dkey_sum = dkey_sum + jnp.einsum(
            "hqk,qhd->khd", grad_score, part_query, preferred_element_type=jnp.float32
        )
        dvalue_sum = dvalue_sum + jnp.einsum(
            "hqk,qhd->khd", weights_half, part_grads, preferred_element_type=jnp.float32
        )
    slot_dquery = jnp.concatenate(query_parts, axis=0).reshape(cluster_rows, head_cols)
    slot_dkey = (dkey_sum * score_scale).astype(jnp.bfloat16).reshape(cluster_rows, head_cols)
    slot_dvalue = dvalue_sum.astype(jnp.bfloat16).reshape(cluster_rows, head_cols)
    back_hit = (slot_source[None, :] == peer_order[:, None]) & filled[None, :]
    back_any = jnp.any(back_hit, axis=1)
    back_slot = jnp.sum(back_hit.astype(jnp.int32) * slot_order[None, :], axis=1)
    share_rows = w_query.shape[0] // lax.axis_size("head")
    total = jnp.einsum("dh,th->dt", w_query, slot_dquery, preferred_element_type=jnp.float32)
    total = total + jnp.einsum("dh,th->dt", w_key, slot_dkey, preferred_element_type=jnp.float32)
    total = total + jnp.einsum(
        "dh,th->dt", w_value, slot_dvalue, preferred_element_type=jnp.float32
    )
    column_share = lax.psum_scatter(
        total.astype(jnp.bfloat16), "head", scatter_dimension=0, tiled=True
    )
    column_share = column_share.reshape(share_rows, slot_count, PAGE)
    picked = jnp.take(column_share, back_slot, axis=1)
    picked = jnp.where(back_any[None, :, None], picked, jnp.zeros_like(picked))
    returned = lax.all_to_all(picked, "tok", split_axis=1, concat_axis=1, tiled=True)
    input_grad = jnp.take(returned, my_clusters, axis=1).reshape(share_rows, tok_rows).T
    return input_grad


MESH = pl.DeviceIdType.MESH
NT = (((1,), (1,)), ((), ()))
TN = (((0,), (0,)), ((), ()))


def dot(a, b, dims):
    return lax.dot_general(a, b, dims, preferred_element_type=jnp.float32)


def whole_kernel(
    sizes, cluster_ref, q_ref, k_ref, v_ref, og_ref, wq_ref, wk_ref, wv_ref, wo_ref, out_ref,
    og_mine, og_other, wq_vm, wk_vm, wv_vm, wo_vm, grads, all_q, all_k, all_v, all_g,
    slot_q, slot_k, slot_v, done_q, done_k, done_v, ret_q, ret_k, ret_v, part_out, part_in, mine, held, value_sum,
    cluster_vm, slot_vm, place_vm, slot_sm, place_sm,
    load_sem, swap_send, swap_recv, fwd_send, fwd_recv, ret_send, ret_recv,
):
    peers, pages, heads, slots = sizes
    width = heads * HEAD_DIM
    rows = pages * PAGE
    scale = HEAD_DIM ** (-0.5)
    me = lax.axis_index("tok")
    group = lax.axis_index("head")
    other = 1 - group
    owners = [peers // 4 + head * (peers // 2) // heads for head in range(heads)]

    loads = [
        pltpu.make_async_copy(og_ref, og_mine, load_sem.at[0]),
        pltpu.make_async_copy(wo_ref, wo_vm, load_sem.at[1]),
        pltpu.make_async_copy(wq_ref, wq_vm, load_sem.at[2]),
        pltpu.make_async_copy(wk_ref, wk_vm, load_sem.at[3]),
        pltpu.make_async_copy(wv_ref, wv_vm, load_sem.at[4]),
    ]
    cluster_load = pltpu.make_async_copy(cluster_ref, cluster_vm, load_sem.at[5])
    cluster_load.start()
    for load in loads:
        load.start()

    is_owner = functools.reduce(lambda a, b: a | b, [me == owner for owner in owners])
    barrier = pltpu.get_barrier_semaphore()
    pl.semaphore_signal(barrier, inc=1, device_id={"head": other}, device_id_type=MESH)
    for peer in range(peers):
        meets = me != peer if peer in owners else is_owner & (me != peer)

        @pl.when(meets)
        def _():
            pl.semaphore_signal(barrier, inc=1, device_id={"tok": peer}, device_id_type=MESH)

    zero_page = jnp.zeros((PAGE, HEAD_DIM), jnp.bfloat16)
    for full in (all_q, all_k, all_v, all_g):
        full[peers * pages] = zero_page
    cluster_load.wait()
    page_total = peers * pages
    square = (page_total, page_total)
    down = lax.broadcasted_iota(jnp.int32, square, 0)
    along = lax.broadcasted_iota(jnp.int32, square, 1)

    def upright(row):
        return jnp.sum(jnp.where(down == along, row, 0), axis=1, keepdims=True)

    cluster_row = cluster_vm[...]
    before = (upright(cluster_row) == cluster_row) & (down < along)
    rank_row = jnp.sum(before.astype(jnp.int32), axis=0, keepdims=True)
    place_row = cluster_row * slots + rank_row
    place_vm[...] = place_row
    shape = (page_total, peers * slots)
    hit = upright(place_row) == lax.broadcasted_iota(jnp.int32, shape, 1)
    missing = lax.broadcasted_iota(jnp.int32, shape, 0) - page_total
    slot_vm[...] = page_total + jnp.sum(jnp.where(hit, missing, 0), axis=0, keepdims=True)
    tables = [
        pltpu.make_async_copy(slot_vm, slot_sm, load_sem.at[6]),
        pltpu.make_async_copy(place_vm, place_sm, load_sem.at[7]),
    ]
    for table in tables:
        table.start()

    @pl.when(is_owner)
    def _():
        pl.semaphore_wait(barrier, peers)

    @pl.when(jnp.logical_not(is_owner))
    def _():
        pl.semaphore_wait(barrier, heads + 1)

    og_swap = pltpu.make_async_remote_copy(
        src_ref=og_ref, dst_ref=og_other, send_sem=swap_send.at[0], recv_sem=swap_recv.at[0],
        device_id={"head": other}, device_id_type=MESH,
    )
    og_swap.start()

    fulls = (all_q, all_k, all_v, all_g)
    sources = (q_ref, k_ref, v_ref, grads)

    def forward(tensor, head):
        piece = sources[tensor].at[:, :, pl.ds(head * HEAD_DIM, HEAD_DIM)]
        spot = fulls[tensor].at[pl.ds(me * pages, pages)]
        local = pltpu.make_async_copy(piece, spot, fwd_recv.at[tensor, me])
        remote = pltpu.make_async_remote_copy(
            src_ref=piece, dst_ref=spot, send_sem=fwd_send.at[tensor, head],
            recv_sem=fwd_recv.at[tensor, me], device_id={"tok": owners[head]}, device_id_type=MESH,
        )
        return local, remote

    def send_forward(tensor):
        for head in (0, 2, 1, 3):
            local, remote = forward(tensor, head)

            @pl.when(me == owners[head])
            def _():
                local.start()

            @pl.when(me != owners[head])
            def _():
                remote.start()

    send_forward(0)
    send_forward(1)

    loads[0].wait()
    loads[1].wait()
    here = pl.ds(pl.multiple_of(group * width, HEAD_DIM), width)
    there = pl.ds(pl.multiple_of(other * width, HEAD_DIM), width)
    grad_sum = dot(og_mine[...].reshape(rows, width), wo_vm[:, here], NT)
    og_swap.wait()
    grad_sum = grad_sum + dot(og_other[...].reshape(rows, width), wo_vm[:, there], NT)
    grads[...] = grad_sum.astype(jnp.bfloat16).reshape(pages, PAGE, width)
    send_forward(3)
    send_forward(2)

    slot_sets = (slot_q, slot_k, slot_v)
    done_sets = (done_q, done_k, done_v)
    ret_sets = (ret_q, ret_k, ret_v)
    cluster_rows = slots * PAGE

    split = pages // CHUNKS

    def give_back(tensor, chunk, head, peer):
        piece = done_sets[tensor].at[pl.ds(peer * pages + chunk * split, split)]
        spot = ret_sets[tensor].at[pl.ds(chunk * split, split), :, pl.ds(head * HEAD_DIM, HEAD_DIM)]
        local = pltpu.make_async_copy(piece, spot, ret_recv.at[tensor, chunk, head])
        remote = pltpu.make_async_remote_copy(
            src_ref=piece, dst_ref=spot, send_sem=ret_send.at[tensor, chunk, peer],
            recv_sem=ret_recv.at[tensor, chunk, head], device_id={"tok": peer}, device_id_type=MESH,
        )
        return local, remote

    def wait_tensor(tensor, head):
        for peer in range(peers):
            piece = sources[tensor].at[:, :, pl.ds(head * HEAD_DIM, HEAD_DIM)]
            spot = fulls[tensor].at[pl.ds(peer * pages, pages)]
            if peer == owners[head]:
                pltpu.make_async_copy(piece, spot, fwd_recv.at[tensor, peer]).wait()
            else:
                pltpu.make_async_remote_copy(
                    src_ref=piece, dst_ref=spot, send_sem=fwd_send.at[tensor, head],
                    recv_sem=fwd_recv.at[tensor, peer], device_id={"tok": peer}, device_id_type=MESH,
                ).wait_recv()

    def gather(full, cluster):
        return jnp.concatenate(
            [full[slot_sm[0, cluster * slots + slot]] for slot in range(slots)], axis=0
        )

    def scatter(slot_set, cluster, value):
        slot_set[pl.ds(cluster * slots, slots)] = value.astype(jnp.bfloat16).reshape(
            slots, PAGE, HEAD_DIM
        )

    def every_cluster(step):
        def body(index, carry):
            for lane in range(UNROLL):
                step(index * UNROLL + lane)
            return carry

        lax.fori_loop(0, peers // UNROLL, body, 0)

    def reorder(tensors):
        def body(peer, carry):
            for inner in range(pages):
                page = peer * pages + inner
                place = place_sm[0, page]
                for tensor in tensors:
                    done_sets[tensor][page] = slot_sets[tensor][place]
            return carry

        lax.fori_loop(0, peers, body, 0)

    def send_back(tensors, chunk, head):
        for peer in sorted(range(peers), key=lambda p: (p % 4, p // 4)):
            for tensor in tensors:
                local, remote = give_back(tensor, chunk, head, peer)
                if peer == owners[head]:
                    local.start()
                else:
                    remote.start()

    def weigh(cluster):
        query, key = gather(all_q, cluster), gather(all_k, cluster)
        row_index = lax.broadcasted_iota(jnp.int32, (cluster_rows, cluster_rows), 0)
        col_index = lax.broadcasted_iota(jnp.int32, (cluster_rows, cluster_rows), 1)
        score = jnp.where(col_index <= row_index, dot(query, key, NT) * scale, -1e30)
        row_max = jnp.max(score, axis=1, keepdims=True)
        raised = jnp.exp(score - row_max)
        held[cluster] = raised * (1.0 / jnp.sum(raised, axis=1, keepdims=True))

    def value_step(cluster):
        scatter(slot_v, cluster, dot(held[cluster].astype(jnp.bfloat16), gather(all_g, cluster), TN))

    def score_step(cluster):
        query, key, value, grad = [gather(full, cluster) for full in fulls]
        weights = held[cluster]
        grad_weights = dot(grad, value, NT)
        row_delta = jnp.sum(weights * grad_weights, axis=1, keepdims=True)
        grad_score = (weights * (grad_weights - row_delta)).astype(jnp.bfloat16)
        scatter(slot_q, cluster, dot(grad_score, key, (((1,), (0,)), ((), ()))) * scale)
        scatter(slot_k, cluster, dot(grad_score, query, TN) * scale)

    def as_owner(todo):
        for head in range(heads):
            @pl.when(me == owners[head])
            def _():
                todo(head)

    for table in tables:
        table.wait()
    as_owner(lambda head: (wait_tensor(0, head), wait_tensor(1, head)))

    @pl.when(is_owner)
    def _():
        every_cluster(weigh)

    as_owner(lambda head: wait_tensor(3, head))

    @pl.when(is_owner)
    def _():
        every_cluster(value_step)
        reorder((2,))

    as_owner(lambda head: wait_tensor(2, head))
    as_owner(lambda head: [send_back((2,), chunk, head) for chunk in range(CHUNKS)])

    @pl.when(is_owner)
    def _():
        every_cluster(score_step)
        reorder((0, 1))

    as_owner(lambda head: [send_back((0, 1), chunk, head) for chunk in range(CHUNKS)])

    def wait_back(tensor, chunk):
        for head in range(heads):
            local, remote = give_back(tensor, chunk, head, owners[head])

            @pl.when(me == owners[head])
            def _():
                local.wait()

            @pl.when(me != owners[head])
            def _():
                remote.wait_recv()

    for load in loads[2:]:
        load.wait()
    chunk_rows = split * PAGE
    for chunk in range(CHUNKS):
        wait_back(2, chunk)
    value_sum[...] = dot(ret_v[...].reshape(rows, width), wv_vm[...], NT)

    swaps = []
    for chunk in range(CHUNKS):
        span = pl.ds(chunk * chunk_rows, chunk_rows)
        wait_back(0, chunk)
        wait_back(1, chunk)
        dquery = ret_q[pl.ds(chunk * split, split)].reshape(chunk_rows, width)
        dkey = ret_k[pl.ds(chunk * split, split)].reshape(chunk_rows, width)

        def partial(half):
            total = dot(dquery, wq_vm[half, :], NT) + dot(dkey, wk_vm[half, :], NT)
            return (total + value_sum[span, half]).astype(jnp.bfloat16)

        part_out[chunk] = partial(there)
        swap = pltpu.make_async_remote_copy(
            src_ref=part_out.at[chunk], dst_ref=part_in.at[chunk],
            send_sem=swap_send.at[1 + chunk], recv_sem=swap_recv.at[1 + chunk],
            device_id={"head": other}, device_id_type=MESH,
        )
        swap.start()
        swaps.append(swap)
        mine[span, :] = partial(here)
    for chunk in range(CHUNKS):
        span = pl.ds(chunk * chunk_rows, chunk_rows)
        swaps[chunk].wait()
        out_ref[span, :] = (
            mine[span, :].astype(jnp.float32) + part_in[chunk].astype(jnp.float32)
        ).astype(jnp.bfloat16)

    for head in range(heads):
        @pl.when(me != owners[head])
        def _():
            for tensor in range(4):
                forward(tensor, head)[1].wait_send()

        @pl.when(me == owners[head])
        def _():
            for peer in range(peers):
                if peer != owners[head]:
                    for tensor in range(3):
                        for chunk in range(CHUNKS):
                            give_back(tensor, chunk, head, peer)[1].wait_send()


def gathered_bytes(peers, rows, heads):
    tokens = peers * rows
    slot_rows = peers * (peers // 2) * PAGE
    weights = peers * ((peers // 2) * PAGE) ** 2 * 4
    return (7 * tokens + 3 * slot_rows) * HEAD_DIM * 2 + weights


def per_device_fast(queries, keys, values, out_grad, w_query, w_key, w_value, w_out, page_cluster):
    rows, width = queries.shape
    pages = rows // PAGE
    heads = width // HEAD_DIM
    peers = lax.axis_size("tok")
    slots = peers // 2
    page_total = page_cluster.shape[0]
    paged = (pages, PAGE, width)
    half = jnp.bfloat16
    full = pltpu.VMEM((page_total + 1, PAGE, HEAD_DIM), half)
    slotted = pltpu.VMEM((peers * slots, PAGE, HEAD_DIM), half)
    done = pltpu.VMEM((page_total, PAGE, HEAD_DIM), half)
    small = pltpu.VMEM(paged, half)
    weight = pltpu.VMEM(w_query.shape, half)
    in_hbm = pl.BlockSpec(memory_space=pltpu.HBM)
    return pl.pallas_call(
        functools.partial(whole_kernel, (peers, pages, heads, slots)),
        out_shape=jax.ShapeDtypeStruct((rows, width), half),
        in_specs=[in_hbm] * 9,
        out_specs=pl.BlockSpec(memory_space=pltpu.VMEM),
        scratch_shapes=[small, small, weight, weight, weight, pltpu.VMEM(w_out.shape, half), small]
        + [full] * 4 + [slotted] * 3 + [done] * 3 + [small] * 3
        + [pltpu.VMEM((CHUNKS, rows // CHUNKS, width), half)] * 2
        + [
            pltpu.VMEM((rows, width), half),
            pltpu.VMEM((peers, slots * PAGE, slots * PAGE), jnp.float32),
            pltpu.VMEM((rows, w_query.shape[0]), jnp.float32),
        ]
        + [pltpu.VMEM((1, size), jnp.int32) for size in (page_total, peers * slots, page_total)]
        + [pltpu.SMEM((1, size), jnp.int32) for size in (peers * slots, page_total)]
        + [
            pltpu.SemaphoreType.DMA((8,)),
            pltpu.SemaphoreType.DMA((1 + CHUNKS,)),
            pltpu.SemaphoreType.DMA((1 + CHUNKS,)),
            pltpu.SemaphoreType.DMA((4, heads)),
            pltpu.SemaphoreType.DMA((4, peers)),
            pltpu.SemaphoreType.DMA((3, CHUNKS, peers)),
            pltpu.SemaphoreType.DMA((3, CHUNKS, heads)),
        ],
        compiler_params=pltpu.CompilerParams(
            collective_id=0, has_side_effects=True, vmem_limit_bytes=VMEM_GRANT
        ),
    )(
        page_cluster.reshape(1, page_total), queries.reshape(paged), keys.reshape(paged), values.reshape(paged),
        out_grad.reshape(paged), w_query, w_key, w_value, w_out,
    )


def choose(*arrays):
    rows, width = arrays[0].shape
    heads = width // HEAD_DIM
    peers = lax.axis_size("tok")
    fits = gathered_bytes(peers, rows, heads) < 24 * 1024 * 1024
    whole_chunks = (rows // PAGE) % CHUNKS == 0 and peers % UNROLL == 0
    if lax.axis_size("head") == 2 and heads > 1 and (peers // 2) % heads == 0 and fits and whole_chunks:
        return per_device_fast(*arrays)
    return per_device(*arrays)


def solution(mesh):
    placed = (
        P("tok", "head"),
        P("tok", "head"),
        P("tok", "head"),
        P("tok", "head"),
        P(None, "head"),
        P(None, "head"),
        P(None, "head"),
        P("head", None),
        P(),
    )
    return jax.shard_map(
        choose, mesh=mesh, in_specs=placed, out_specs=P("tok", "head"), check_vma=False
    )
```

```python
import functools

import jax
import jax.numpy as jnp
from jax import lax
from jax.experimental import pallas as pl
from jax.experimental.pallas import tpu as pltpu
from jax.sharding import PartitionSpec as P

HEAD_DIM = 128
PAGE = 32
CHUNKS = 3
UNROLL = 4
VMEM_GRANT = 67043328


def per_device(queries, keys, values, out_grad, w_query, w_key, w_value, w_out, page_cluster):
    tok_rows, head_cols = queries.shape
    pages_here = tok_rows // PAGE
    heads_here = head_cols // HEAD_DIM
    peers = lax.axis_size("tok")
    myself = lax.axis_index("tok")
    page_total = page_cluster.shape[0]
    slot_count = peers // 2
    cluster_rows = slot_count * PAGE
    score_scale = HEAD_DIM ** (-0.5)
    grad_heads = jnp.einsum(
        "td,hd->th",
        lax.all_gather(out_grad, "head", axis=1, tiled=True),
        w_out,
        preferred_element_type=jnp.float32,
    ).astype(jnp.bfloat16)
    page_order = jnp.arange(page_total, dtype=jnp.int32)
    peer_order = jnp.arange(peers, dtype=jnp.int32)
    cluster_onehot = (page_cluster[:, None] == peer_order[None, :]).astype(jnp.int32)
    running_count = jnp.cumsum(cluster_onehot, axis=0) - cluster_onehot
    page_rank = jnp.sum(running_count * cluster_onehot, axis=1)
    my_clusters = lax.dynamic_slice_in_dim(page_cluster, myself * pages_here, pages_here)
    going = my_clusters[None, :] == peer_order[:, None]
    going_any = jnp.any(going, axis=1)
    going_index = jnp.sum(
        going.astype(jnp.int32) * jnp.arange(pages_here, dtype=jnp.int32)[None, :], axis=1
    )

    def outgoing(matrix):
        paged = matrix.reshape(pages_here, PAGE, matrix.shape[1])
        picked = jnp.take(paged, going_index, axis=0)
        return jnp.where(going_any[:, None, None], picked, jnp.zeros_like(picked))

    arrived = (
        lax.all_to_all(outgoing(queries), "tok", split_axis=0, concat_axis=0, tiled=True),
        lax.all_to_all(outgoing(keys), "tok", split_axis=0, concat_axis=0, tiled=True),
        lax.all_to_all(outgoing(values), "tok", split_axis=0, concat_axis=0, tiled=True),
        lax.all_to_all(outgoing(grad_heads), "tok", split_axis=0, concat_axis=0, tiled=True),
    )
    slot_order = jnp.arange(slot_count, dtype=jnp.int32)
    slot_hit = (page_cluster[None, :] == myself) & (page_rank[None, :] == slot_order[:, None])
    filled = jnp.any(slot_hit, axis=1)
    slot_page = jnp.sum(slot_hit.astype(jnp.int32) * page_order[None, :], axis=1)
    slot_source = slot_page // pages_here

    def assemble(matrix):
        picked = jnp.take(matrix, slot_source, axis=0)
        picked = jnp.where(filled[:, None, None], picked, jnp.zeros_like(picked))
        return picked.reshape(cluster_rows, heads_here, HEAD_DIM)

    slot_query = assemble(arrived[0])
    slot_keys = assemble(arrived[1])
    slot_values = assemble(arrived[2])
    slot_grads = assemble(arrived[3])
    inner_index = jnp.arange(PAGE, dtype=jnp.int32)
    key_pos = (slot_page[:, None] * PAGE + inner_index[None, :]).reshape(cluster_rows)
    key_live = jnp.broadcast_to(filled[:, None], (slot_count, PAGE)).reshape(cluster_rows)
    key_order = jnp.arange(cluster_rows, dtype=jnp.int32)
    block_rows = min(512, cluster_rows)
    dkey_sum = jnp.zeros((cluster_rows, heads_here, HEAD_DIM), jnp.float32)
    dvalue_sum = jnp.zeros((cluster_rows, heads_here, HEAD_DIM), jnp.float32)
    query_parts = []
    for block_index in range(cluster_rows // block_rows):
        first_row = block_index * block_rows
        last_row = first_row + block_rows
        part_query = slot_query[first_row:last_row]
        part_grads = slot_grads[first_row:last_row]
        row_pos = key_pos[first_row:last_row]
        row_order = key_order[first_row:last_row]
        allowed = key_live[None, :] & (key_pos[None, :] <= row_pos[:, None]) | (
            key_order[None, :] == row_order[:, None]
        )
        score = (
            jnp.einsum("qhd,khd->hqk", part_query, slot_keys, preferred_element_type=jnp.float32)
            * score_scale
        )
        score = jnp.where(allowed[None], score, -1e30)
        row_max = jnp.max(score, axis=2, keepdims=True)
        raised = jnp.where(allowed[None], jnp.exp(score - row_max), 0.0)
        weights = raised / jnp.sum(raised, axis=2, keepdims=True)
        weights_half = weights.astype(jnp.bfloat16)
        grad_weights = jnp.einsum(
            "qhd,khd->hqk", part_grads, slot_values, preferred_element_type=jnp.float32
        )
        row_delta = jnp.sum(weights * grad_weights, axis=2, keepdims=True)
        grad_score = (weights * (grad_weights - row_delta)).astype(jnp.bfloat16)
        grad_query = (
            jnp.einsum("hqk,khd->qhd", grad_score, slot_keys, preferred_element_type=jnp.float32)
            * score_scale
        )
        query_parts.append(grad_query.astype(jnp.bfloat16))
        dkey_sum = dkey_sum + jnp.einsum(
            "hqk,qhd->khd", grad_score, part_query, preferred_element_type=jnp.float32
        )
        dvalue_sum = dvalue_sum + jnp.einsum(
            "hqk,qhd->khd", weights_half, part_grads, preferred_element_type=jnp.float32
        )
    slot_dquery = jnp.concatenate(query_parts, axis=0).reshape(cluster_rows, head_cols)
    slot_dkey = (dkey_sum * score_scale).astype(jnp.bfloat16).reshape(cluster_rows, head_cols)
    slot_dvalue = dvalue_sum.astype(jnp.bfloat16).reshape(cluster_rows, head_cols)
    back_hit = (slot_source[None, :] == peer_order[:, None]) & filled[None, :]
    back_any = jnp.any(back_hit, axis=1)
    back_slot = jnp.sum(back_hit.astype(jnp.int32) * slot_order[None, :], axis=1)
    share_rows = w_query.shape[0] // lax.axis_size("head")
    total = jnp.einsum("dh,th->dt", w_query, slot_dquery, preferred_element_type=jnp.float32)
    total = total + jnp.einsum("dh,th->dt", w_key, slot_dkey, preferred_element_type=jnp.float32)
    total = total + jnp.einsum(
        "dh,th->dt", w_value, slot_dvalue, preferred_element_type=jnp.float32
    )
    column_share = lax.psum_scatter(
        total.astype(jnp.bfloat16), "head", scatter_dimension=0, tiled=True
    )
    column_share = column_share.reshape(share_rows, slot_count, PAGE)
    picked = jnp.take(column_share, back_slot, axis=1)
    picked = jnp.where(back_any[None, :, None], picked, jnp.zeros_like(picked))
    returned = lax.all_to_all(picked, "tok", split_axis=1, concat_axis=1, tiled=True)
    input_grad = jnp.take(returned, my_clusters, axis=1).reshape(share_rows, tok_rows).T
    return input_grad


MESH = pl.DeviceIdType.MESH
NT = (((1,), (1,)), ((), ()))
TN = (((0,), (0,)), ((), ()))


def dot(a, b, dims):
    return lax.dot_general(a, b, dims, preferred_element_type=jnp.float32)


def whole_kernel(
    sizes, cluster_ref, q_ref, k_ref, v_ref, og_ref, wq_ref, wk_ref, wv_ref, wo_ref, out_ref,
    og_mine, og_other, wq_vm, wk_vm, wv_vm, wo_vm, grads, all_q, all_k, all_v, all_g,
    slot_q, slot_k, slot_v, done_q, done_k, done_v, ret_q, ret_k, ret_v, part_out, part_in, mine, held, value_sum,
    cluster_vm, slot_vm, place_vm, slot_sm, place_sm,
    load_sem, swap_send, swap_recv, fwd_send, fwd_recv, ret_send, ret_recv,
):
    peers, pages, heads, slots = sizes
    width = heads * HEAD_DIM
    rows = pages * PAGE
    scale = HEAD_DIM ** (-0.5)
    me = lax.axis_index("tok")
    group = lax.axis_index("head")
    other = 1 - group
    owners = [peers // 4 + head * (peers // 2) // heads for head in range(heads)]

    loads = [
        pltpu.make_async_copy(og_ref, og_mine, load_sem.at[0]),
        pltpu.make_async_copy(wo_ref, wo_vm, load_sem.at[1]),
        pltpu.make_async_copy(wq_ref, wq_vm, load_sem.at[2]),
        pltpu.make_async_copy(wk_ref, wk_vm, load_sem.at[3]),
        pltpu.make_async_copy(wv_ref, wv_vm, load_sem.at[4]),
    ]
    cluster_load = pltpu.make_async_copy(cluster_ref, cluster_vm, load_sem.at[5])
    cluster_load.start()
    for load in loads:
        load.start()

    is_owner = functools.reduce(lambda a, b: a | b, [me == owner for owner in owners])
    barrier = pltpu.get_barrier_semaphore()
    pl.semaphore_signal(barrier, inc=1, device_id={"head": other}, device_id_type=MESH)
    for peer in range(peers):
        meets = me != peer if peer in owners else is_owner & (me != peer)

        @pl.when(meets)
        def _():
            pl.semaphore_signal(barrier, inc=1, device_id={"tok": peer}, device_id_type=MESH)

    zero_page = jnp.zeros((PAGE, HEAD_DIM), jnp.bfloat16)
    for full in (all_q, all_k, all_v, all_g):
        full[peers * pages] = zero_page
    cluster_load.wait()
    page_total = peers * pages
    square = (page_total, page_total)
    down = lax.broadcasted_iota(jnp.int32, square, 0)
    along = lax.broadcasted_iota(jnp.int32, square, 1)

    def upright(row):
        return jnp.sum(jnp.where(down == along, row, 0), axis=1, keepdims=True)

    cluster_row = cluster_vm[...]
    before = (upright(cluster_row) == cluster_row) & (down < along)
    rank_row = jnp.sum(before.astype(jnp.int32), axis=0, keepdims=True)
    place_row = cluster_row * slots + rank_row
    place_vm[...] = place_row
    shape = (page_total, peers * slots)
    hit = upright(place_row) == lax.broadcasted_iota(jnp.int32, shape, 1)
    missing = lax.broadcasted_iota(jnp.int32, shape, 0) - page_total
    slot_vm[...] = page_total + jnp.sum(jnp.where(hit, missing, 0), axis=0, keepdims=True)
    tables = [
        pltpu.make_async_copy(slot_vm, slot_sm, load_sem.at[6]),
        pltpu.make_async_copy(place_vm, place_sm, load_sem.at[7]),
    ]
    for table in tables:
        table.start()

    @pl.when(is_owner)
    def _():
        pl.semaphore_wait(barrier, peers)

    @pl.when(jnp.logical_not(is_owner))
    def _():
        pl.semaphore_wait(barrier, heads + 1)

    og_swap = pltpu.make_async_remote_copy(
        src_ref=og_ref, dst_ref=og_other, send_sem=swap_send.at[0], recv_sem=swap_recv.at[0],
        device_id={"head": other}, device_id_type=MESH,
    )
    og_swap.start()

    fulls = (all_q, all_k, all_v, all_g)
    sources = (q_ref, k_ref, v_ref, grads)

    def forward(tensor, head):
        piece = sources[tensor].at[:, :, pl.ds(head * HEAD_DIM, HEAD_DIM)]
        spot = fulls[tensor].at[pl.ds(me * pages, pages)]
        local = pltpu.make_async_copy(piece, spot, fwd_recv.at[tensor, me])
        remote = pltpu.make_async_remote_copy(
            src_ref=piece, dst_ref=spot, send_sem=fwd_send.at[tensor, head],
            recv_sem=fwd_recv.at[tensor, me], device_id={"tok": owners[head]}, device_id_type=MESH,
        )
        return local, remote

    def send_forward(tensor):
        for head in sorted(range(heads), key=lambda head: head % 2):
            local, remote = forward(tensor, head)

            @pl.when(me == owners[head])
            def _():
                local.start()

            @pl.when(me != owners[head])
            def _():
                remote.start()

    send_forward(0)
    send_forward(1)

    loads[0].wait()
    loads[1].wait()
    here = pl.ds(pl.multiple_of(group * width, HEAD_DIM), width)
    there = pl.ds(pl.multiple_of(other * width, HEAD_DIM), width)
    grad_sum = dot(og_mine[...].reshape(rows, width), wo_vm[:, here], NT)
    og_swap.wait()
    grad_sum = grad_sum + dot(og_other[...].reshape(rows, width), wo_vm[:, there], NT)
    grads[...] = grad_sum.astype(jnp.bfloat16).reshape(pages, PAGE, width)
    send_forward(3)
    send_forward(2)

    slot_sets = (slot_q, slot_k, slot_v)
    done_sets = (done_q, done_k, done_v)
    ret_sets = (ret_q, ret_k, ret_v)
    cluster_rows = slots * PAGE

    split = pages // CHUNKS

    def give_back(tensor, chunk, head, peer):
        piece = done_sets[tensor].at[pl.ds(peer * pages + chunk * split, split)]
        spot = ret_sets[tensor].at[pl.ds(chunk * split, split), :, pl.ds(head * HEAD_DIM, HEAD_DIM)]
        local = pltpu.make_async_copy(piece, spot, ret_recv.at[tensor, chunk, head])
        remote = pltpu.make_async_remote_copy(
            src_ref=piece, dst_ref=spot, send_sem=ret_send.at[tensor, chunk, peer],
            recv_sem=ret_recv.at[tensor, chunk, head], device_id={"tok": peer}, device_id_type=MESH,
        )
        return local, remote

    def wait_tensor(tensor, head):
        for peer in range(peers):
            piece = sources[tensor].at[:, :, pl.ds(head * HEAD_DIM, HEAD_DIM)]
            spot = fulls[tensor].at[pl.ds(peer * pages, pages)]
            if peer == owners[head]:
                pltpu.make_async_copy(piece, spot, fwd_recv.at[tensor, peer]).wait()
            else:
                pltpu.make_async_remote_copy(
                    src_ref=piece, dst_ref=spot, send_sem=fwd_send.at[tensor, head],
                    recv_sem=fwd_recv.at[tensor, peer], device_id={"tok": peer}, device_id_type=MESH,
                ).wait_recv()

    def gather(full, cluster):
        return jnp.concatenate(
            [full[slot_sm[0, cluster * slots + slot]] for slot in range(slots)], axis=0
        )

    def scatter(slot_set, cluster, value):
        slot_set[pl.ds(cluster * slots, slots)] = value.astype(jnp.bfloat16).reshape(
            slots, PAGE, HEAD_DIM
        )

    def every_cluster(step):
        def body(index, carry):
            for lane in range(UNROLL):
                step(index * UNROLL + lane)
            return carry

        lax.fori_loop(0, peers // UNROLL, body, 0)

    def reorder(tensors):
        def body(peer, carry):
            for inner in range(pages):
                page = peer * pages + inner
                place = place_sm[0, page]
                for tensor in tensors:
                    done_sets[tensor][page] = slot_sets[tensor][place]
            return carry

        lax.fori_loop(0, peers, body, 0)

    def send_back(tensors, chunk, head):
        for peer in sorted(range(peers), key=lambda peer: (peer % heads, -abs(peer - owners[head]))):
            for tensor in tensors:
                local, remote = give_back(tensor, chunk, head, peer)
                if peer == owners[head]:
                    local.start()
                else:
                    remote.start()

    def weigh(cluster):
        query, key = gather(all_q, cluster), gather(all_k, cluster)
        row_index = lax.broadcasted_iota(jnp.int32, (cluster_rows, cluster_rows), 0)
        col_index = lax.broadcasted_iota(jnp.int32, (cluster_rows, cluster_rows), 1)
        score = jnp.where(col_index <= row_index, dot(query, key, NT) * scale, -1e30)
        row_max = jnp.max(score, axis=1, keepdims=True)
        raised = jnp.exp(score - row_max)
        held[cluster] = raised * (1.0 / jnp.sum(raised, axis=1, keepdims=True))

    def value_step(cluster):
        scatter(slot_v, cluster, dot(held[cluster].astype(jnp.bfloat16), gather(all_g, cluster), TN))

    def score_step(cluster):
        query, key, value, grad = [gather(full, cluster) for full in fulls]
        weights = held[cluster]
        grad_weights = dot(grad, value, NT)
        row_delta = jnp.sum(weights * grad_weights, axis=1, keepdims=True)
        grad_score = (weights * (grad_weights - row_delta)).astype(jnp.bfloat16)
        scatter(slot_q, cluster, dot(grad_score, key, (((1,), (0,)), ((), ()))) * scale)
        scatter(slot_k, cluster, dot(grad_score, query, TN) * scale)

    def as_owner(todo):
        for head in range(heads):
            @pl.when(me == owners[head])
            def _():
                todo(head)

    for table in tables:
        table.wait()
    as_owner(lambda head: (wait_tensor(0, head), wait_tensor(1, head)))

    @pl.when(is_owner)
    def _():
        every_cluster(weigh)

    as_owner(lambda head: wait_tensor(3, head))

    @pl.when(is_owner)
    def _():
        every_cluster(value_step)
        reorder((2,))

    as_owner(lambda head: wait_tensor(2, head))
    as_owner(lambda head: [send_back((2,), chunk, head) for chunk in range(CHUNKS)])

    @pl.when(is_owner)
    def _():
        every_cluster(score_step)
        reorder((0, 1))

    as_owner(lambda head: [send_back((0, 1), chunk, head) for chunk in range(CHUNKS)])

    def wait_back(tensor, chunk):
        for head in range(heads):
            local, remote = give_back(tensor, chunk, head, owners[head])

            @pl.when(me == owners[head])
            def _():
                local.wait()

            @pl.when(me != owners[head])
            def _():
                remote.wait_recv()

    for load in loads[2:]:
        load.wait()
    chunk_rows = split * PAGE
    for chunk in range(CHUNKS):
        wait_back(2, chunk)
    value_sum[...] = dot(ret_v[...].reshape(rows, width), wv_vm[...], NT)

    swaps = []
    for chunk in range(CHUNKS):
        span = pl.ds(chunk * chunk_rows, chunk_rows)
        wait_back(0, chunk)
        wait_back(1, chunk)
        dquery = ret_q[pl.ds(chunk * split, split)].reshape(chunk_rows, width)
        dkey = ret_k[pl.ds(chunk * split, split)].reshape(chunk_rows, width)

        def partial(half):
            total = dot(dquery, wq_vm[half, :], NT) + dot(dkey, wk_vm[half, :], NT)
            return (total + value_sum[span, half]).astype(jnp.bfloat16)

        part_out[chunk] = partial(there)
        swap = pltpu.make_async_remote_copy(
            src_ref=part_out.at[chunk], dst_ref=part_in.at[chunk],
            send_sem=swap_send.at[1 + chunk], recv_sem=swap_recv.at[1 + chunk],
            device_id={"head": other}, device_id_type=MESH,
        )
        swap.start()
        swaps.append(swap)
        mine[span, :] = partial(here)
    for chunk in range(CHUNKS):
        span = pl.ds(chunk * chunk_rows, chunk_rows)
        swaps[chunk].wait()
        out_ref[span, :] = (
            mine[span, :].astype(jnp.float32) + part_in[chunk].astype(jnp.float32)
        ).astype(jnp.bfloat16)

    for head in range(heads):
        @pl.when(me != owners[head])
        def _():
            for tensor in range(4):
                forward(tensor, head)[1].wait_send()

        @pl.when(me == owners[head])
        def _():
            for peer in range(peers):
                if peer != owners[head]:
                    for tensor in range(3):
                        for chunk in range(CHUNKS):
                            give_back(tensor, chunk, head, peer)[1].wait_send()


def gathered_bytes(peers, rows, heads):
    tokens = peers * rows
    slot_rows = peers * (peers // 2) * PAGE
    weights = peers * ((peers // 2) * PAGE) ** 2 * 4
    return (7 * tokens + 3 * slot_rows) * HEAD_DIM * 2 + weights


def per_device_fast(queries, keys, values, out_grad, w_query, w_key, w_value, w_out, page_cluster):
    rows, width = queries.shape
    pages = rows // PAGE
    heads = width // HEAD_DIM
    peers = lax.axis_size("tok")
    slots = peers // 2
    page_total = page_cluster.shape[0]
    paged = (pages, PAGE, width)
    half = jnp.bfloat16
    full = pltpu.VMEM((page_total + 1, PAGE, HEAD_DIM), half)
    slotted = pltpu.VMEM((peers * slots, PAGE, HEAD_DIM), half)
    done = pltpu.VMEM((page_total, PAGE, HEAD_DIM), half)
    small = pltpu.VMEM(paged, half)
    weight = pltpu.VMEM(w_query.shape, half)
    in_hbm = pl.BlockSpec(memory_space=pltpu.HBM)
    return pl.pallas_call(
        functools.partial(whole_kernel, (peers, pages, heads, slots)),
        out_shape=jax.ShapeDtypeStruct((rows, width), half),
        in_specs=[in_hbm] * 9,
        out_specs=pl.BlockSpec(memory_space=pltpu.VMEM),
        scratch_shapes=[small, small, weight, weight, weight, pltpu.VMEM(w_out.shape, half), small]
        + [full] * 4 + [slotted] * 3 + [done] * 3 + [small] * 3
        + [pltpu.VMEM((CHUNKS, rows // CHUNKS, width), half)] * 2
        + [
            pltpu.VMEM((rows, width), half),
            pltpu.VMEM((peers, slots * PAGE, slots * PAGE), jnp.float32),
            pltpu.VMEM((rows, w_query.shape[0]), jnp.float32),
        ]
        + [pltpu.VMEM((1, size), jnp.int32) for size in (page_total, peers * slots, page_total)]
        + [pltpu.SMEM((1, size), jnp.int32) for size in (peers * slots, page_total)]
        + [
            pltpu.SemaphoreType.DMA((8,)),
            pltpu.SemaphoreType.DMA((1 + CHUNKS,)),
            pltpu.SemaphoreType.DMA((1 + CHUNKS,)),
            pltpu.SemaphoreType.DMA((4, heads)),
            pltpu.SemaphoreType.DMA((4, peers)),
            pltpu.SemaphoreType.DMA((3, CHUNKS, peers)),
            pltpu.SemaphoreType.DMA((3, CHUNKS, heads)),
        ],
        compiler_params=pltpu.CompilerParams(
            collective_id=0, has_side_effects=True, vmem_limit_bytes=VMEM_GRANT
        ),
    )(
        page_cluster.reshape(1, page_total), queries.reshape(paged), keys.reshape(paged), values.reshape(paged),
        out_grad.reshape(paged), w_query, w_key, w_value, w_out,
    )


def choose(*arrays):
    rows, width = arrays[0].shape
    heads = width // HEAD_DIM
    peers = lax.axis_size("tok")
    fits = gathered_bytes(peers, rows, heads) < 24 * 1024 * 1024
    whole_chunks = (rows // PAGE) % CHUNKS == 0 and peers % UNROLL == 0
    if lax.axis_size("head") == 2 and heads > 1 and (peers // 2) % heads == 0 and fits and whole_chunks:
        return per_device_fast(*arrays)
    return per_device(*arrays)


def solution(mesh):
    placed = (
        P("tok", "head"),
        P("tok", "head"),
        P("tok", "head"),
        P("tok", "head"),
        P(None, "head"),
        P(None, "head"),
        P(None, "head"),
        P("head", None),
        P(),
    )
    return jax.shard_map(
        choose, mesh=mesh, in_specs=placed, out_specs=P("tok", "head"), check_vma=False
    )
```
